256 devices in a mesh: mom: 64 (over z, y, core), tm: 4 (over x).
Axes of the slice: x: 4, y: 4, z: 8, core: 2. Of those that a mesh axis runs over, the one named last changes fastest.
Arguments:
- hist_lesser: float32 [2, 256, 16, 2048], P(None, 'mom', None, 'tm'), may hold values from -2 to 6
- hist_retarded: float32 [2, 256, 16, 2048], P(None, 'mom', None, 'tm'), may hold values from -4 to 4
- propagator: float32 [2, 256, 16, 16], P(None, 'mom'), may hold values from -0.5 to 1.5
- coupling: float32 [256], replicated, may hold values from 0.15 to 0.4
- mf_weight: float32 [256], replicated, may hold values from 0.5 to 2
- lag_weight: float32 [8], replicated, may hold values from 0.05 to 0.2
Outputs:
- new_slice: float32 [2, 256, 16, 2048], P(None, 'mom', None, 'tm')
The draws below stay inside these ranges and needn't reach their ends.
All inputs are finite; a program needn't handle non-finite values.
Results may differ from the reference program's by a relative error of at most 0.0003.
Values sent between devices are 32-bit elements; how exact they have to be, the bound alone decides.
A program may use at most 64 MiB of HBM per device.

```python
import math
import jax
import jax.numpy as jnp
from jax import lax

KX = 16
KY = 16
ORB = 16
W = 8
PASSES = 3
K = 256
H = 128


def draw_hist_lesser(key, part):
    base_key = jax.random.fold_in(key, 11)
    noise_key, rough_key = jax.random.split(base_key)
    shape = (2, K, ORB, H * ORB)
    base = jnp.clip(0.5 * jax.random.normal(noise_key, shape, jnp.float32), -2.0, 2.0)
    lowest = 0.5
    rough = jax.random.uniform(rough_key, (K, ORB, 1), jnp.float32, 0.7, 1.3)
    level = lowest + jnp.arange(K, dtype=jnp.float32) / (K - 1)
    column = jnp.arange(H * ORB, dtype=jnp.int32)
    orbital = jnp.arange(ORB, dtype=jnp.int32)
    marked = ((column[None, :] // ORB == H - 1) & (column[None, :] % ORB == orbital[:, None])).astype(jnp.float32)
    lifted = level[:, None, None] * rough * marked[None, :, :]
    return base.at[1].add(lifted)


def draw_propagator(key, part):
    noise_key = jax.random.fold_in(key, 23)
    shape = (2, K, ORB, ORB)
    noise = jnp.clip(0.1 * jax.random.normal(noise_key, shape, jnp.float32), -0.5, 0.5)
    identity = jnp.eye(ORB, dtype=jnp.float32)
    return noise.at[0].add(identity[None, :, :])


def level_of(key, shape, shards, low, largest):
    def one(position, blocks):
        draws = jax.random.uniform(jax.random.fold_in(jax.random.fold_in(key, 6), position), (blocks,), jnp.float32, low / len(shards), largest / len(shards))
        return jnp.repeat(jnp.exp(draws), shape[position] // blocks).reshape((-1,) + (1,) * (len(shape) - position - 1))

    loudness = one(*shards[0])
    for cut in shards[1:]:
        loudness = loudness * one(*cut)
    return loudness


def centred(stream_key, shape, scale, most, cuts=(), kind=jnp.bfloat16):
    gain = level_of(stream_key, shape, cuts, -0.22, 0.18) if cuts else 1.0
    drawn = jax.random.normal(stream_key, shape, jnp.float32) * scale * gain
    return jnp.minimum(jnp.maximum(drawn, -most), most).astype(kind)


def setup_inputs(seed: int = 0) -> dict:
    key_of = jax.random.split(jax.random.key(seed), 7)
    return {
        "hist_lesser": draw_hist_lesser(jax.random.fold_in(key_of[6], 71), 0),
        "hist_retarded": centred(key_of[1], (2, K, ORB, H * ORB), 1.0, 4.0, ((1, 64), (3, 4)), jnp.float32),
        "propagator": draw_propagator(jax.random.fold_in(key_of[6], 71), 0),
        "coupling": jnp.clip(jnp.exp(jax.random.uniform(key_of[3], (ORB * ORB,), jnp.float32, math.log(0.15), math.log(0.4))), 0.15, 0.4),
        "mf_weight": jnp.clip(jnp.exp(jax.random.uniform(key_of[4], (ORB * ORB,), jnp.float32, math.log(0.5), math.log(2.0))), 0.5, 2.0),
        "lag_weight": jnp.clip(jnp.exp(jax.random.uniform(key_of[5], (W,), jnp.float32, math.log(0.05), math.log(0.2))), 0.05, 0.2),
    }


HIGHEST = lax.Precision.HIGHEST

def momentum_tables():
    index = jnp.arange(KX * KY, dtype=jnp.int32)
    first = index // KY
    second = index % KY
    turn_x = first[:, None] * first[None, :] % KX
    turn_y = second[:, None] * second[None, :] % KY
    phase = 2.0 * math.pi * (turn_x.astype(jnp.float32) / KX + turn_y.astype(jnp.float32) / KY)
    scale = 1.0 / math.sqrt(KX * KY)
    return (jnp.cos(phase) * scale, jnp.sin(phase) * scale)

def complex_product(pattern, first, second):
    real = jnp.einsum(pattern, first[0], second[0], precision=HIGHEST) - jnp.einsum(pattern, first[1], second[1], precision=HIGHEST)
    imaginary = jnp.einsum(pattern, first[0], second[1], precision=HIGHEST) + jnp.einsum(pattern, first[1], second[0], precision=HIGHEST)
    return jnp.stack([real, imaginary])

def back_to_momenta(real, imaginary, cosine, sine):
    out_real = jnp.einsum('rk,rabm->kabm', cosine, real, precision=HIGHEST) + jnp.einsum('rk,rabm->kabm', sine, imaginary, precision=HIGHEST)
    out_imag = jnp.einsum('rk,rabm->kabm', cosine, imaginary, precision=HIGHEST) - jnp.einsum('rk,rabm->kabm', sine, real, precision=HIGHEST)
    return jnp.stack([out_real, out_imag])

def reference(hist_lesser, hist_retarded, propagator, coupling, mf_weight, lag_weight):
    cosine, sine = momentum_tables()
    lesser = hist_lesser.reshape(2, K, ORB, H, ORB)
    retarded = hist_retarded.reshape(2, K, ORB, H, ORB)
    start = complex_product('kab,kbjc->kajc', propagator, lesser)
    zeros = jnp.zeros((2, K, ORB, W - 1, ORB), jnp.float32)
    padded_r = jnp.concatenate([zeros, retarded], axis=3)
    padded_l = jnp.concatenate([zeros, lesser], axis=3)
    strength = (coupling * coupling).reshape(ORB, ORB, 1)
    mean_weight = mf_weight.reshape(ORB, ORB)
    last_mark = (jnp.arange(W) == W - 1).astype(jnp.float32)
    current = start
    for sweep in range(PASSES):
        window = jnp.transpose(current[:, :, :, H - W:, :], (0, 1, 2, 4, 3))
        space_real = jnp.einsum('rk,kabm->rabm', cosine, window[0], precision=HIGHEST) - jnp.einsum('rk,kabm->rabm', sine, window[1], precision=HIGHEST)
        space_imag = jnp.einsum('rk,kabm->rabm', cosine, window[1], precision=HIGHEST) + jnp.einsum('rk,kabm->rabm', sine, window[0], precision=HIGHEST)
        magnitude = strength * (space_real * space_real + space_imag * space_imag)
        lesser_k = back_to_momenta(magnitude * space_real, magnitude * space_imag, cosine, sine)
        pair_k = back_to_momenta(strength * (space_real * space_real - space_imag * space_imag), strength * 2.0 * space_real * space_imag, cosine, sine)
        occupation = lax.optimization_barrier(jnp.mean(window[..., W - 1], axis=1))
        sigma = lesser_k + (mean_weight * occupation)[:, None, :, :, None] * last_mark

        def add_lag(offset, total):
            offset = jnp.asarray(offset).astype(jnp.int32)
            part_r = lax.dynamic_slice_in_dim(padded_r, offset, H, 3)
            part_l = lax.dynamic_slice_in_dim(padded_l, offset, H, 3)
            sigma_lag = lax.dynamic_index_in_dim(sigma, offset, 4, keepdims=False)
            pair_lag = lax.dynamic_index_in_dim(pair_k, offset, 4, keepdims=False)
            weight = lax.dynamic_index_in_dim(lag_weight, offset, 0, keepdims=False)
            terms = complex_product('kab,kbjc->kajc', sigma_lag, part_r) + complex_product('kab,kbjc->kajc', pair_lag, part_l)
            return total + weight * terms
        collision = lax.fori_loop(0, W, add_lag, jnp.zeros_like(start))
        current = start + jnp.stack([collision[1], -collision[0]])
    return current.reshape(2, K, ORB, H * ORB)
```

```python
import functools
import math

import jax
import jax.numpy as jnp
import ml_dtypes
import numpy as np
from jax import lax
from jax.experimental import pallas as pl
from jax.experimental.pallas import tpu as pltpu
from jax.sharding import PartitionSpec as P

KX = 16
KY = 16
ORB = 16
W = 8
PASSES = 3
NZ, NY = 8, 4
CHIPS = NZ * NY
TM = 4
HERE = 4
LANES = W * ORB
HALF = LANES // 2
BLOCKS = 4

MESH = pl.DeviceIdType.MESH
F32 = jnp.float32
BF16 = jnp.bfloat16


def momentum_table():
    place = np.arange(KX * KY)
    core, chip, here = place // 128, place // 4 % 32, place % 4
    k = 8 * chip + 4 * core + here
    kx, ky = k // KY, k % KY
    turn = (kx[:, None] * kx[None, :]) % KX + (ky[:, None] * ky[None, :]) % KY
    phase = 2.0 * math.pi * turn / 16.0
    full = np.concatenate([np.cos(phase), np.sin(phase)], axis=1) / 16.0
    full = full.astype(np.float32)
    high = full.astype(ml_dtypes.bfloat16)
    low = (full - high.astype(np.float32)).astype(ml_dtypes.bfloat16)
    return np.stack([high, low])


def split(x):
    high = x.astype(BF16)
    return high, (x - high.astype(F32)).astype(BF16)


def mm(a, b):
    return jnp.dot(a, b, preferred_element_type=F32)


def kernel(
    hl, hr, prop, coup, mf, lag, table,
    out,
    hlv, hrv, wl, wr, tab, startv, startw, hank, sendf, fbuf, sendb, rbuf,
    load_sem, x_send, x_recv, f_send, f_recv, f_own, s_send, s_recv, b_send, b_recv,
):
    dev = lax.axis_index("mom")
    x = lax.axis_index("tm")
    core = lax.rem(dev, 2)
    chip = dev // 2
    z = chip // NY
    y = lax.rem(chip, NY)
    row = chip // 2
    half = lax.rem(chip, 2)

    def peer_chip(dz, dy):
        return lax.rem(z + dz, NZ) * NY + lax.rem(y + dy, NY)

    offsets = [(dz, dy) for dz in (4, 3, 5, 2, 6, 1, 7, 0) for dy in (2, 1, 3, 0) if dz or dy]

    barrier = pltpu.get_barrier_semaphore()
    for dx in (1, 2, 3):
        pl.semaphore_signal(
            barrier, inc=1, device_id={"mom": dev, "tm": lax.rem(x + dx, TM)}, device_id_type=MESH
        )
    for dz, dy in offsets:
        pl.semaphore_signal(
            barrier, inc=1, device_id={"mom": peer_chip(dz, dy) * 2 + core, "tm": x},
            device_id_type=MESH,
        )
    pl.semaphore_signal(
        barrier, inc=1, device_id={"mom": chip * 2 + 1 - core, "tm": x}, device_id_type=MESH
    )

    loads = [
        pltpu.make_async_copy(hl, hlv.at[:, :, :, pl.ds(LANES, BLOCKS * LANES)], load_sem.at[0]),
        pltpu.make_async_copy(hr, hrv.at[:, :, :, pl.ds(LANES, BLOCKS * LANES)], load_sem.at[1]),
        pltpu.make_async_copy(table, tab, load_sem.at[2]),
    ]
    for load in loads:
        load.start()

    own_window = [
        pltpu.make_async_copy(hl.at[:, :, :, pl.ds(2 * LANES, 2 * LANES)], wl, load_sem.at[3]),
        pltpu.make_async_copy(hr.at[:, :, :, pl.ds(2 * LANES, 2 * LANES)], wr, load_sem.at[4]),
    ]

    @pl.when(x == TM - 1)
    def _():
        for copy in own_window:
            copy.start()

    pl.semaphore_wait(barrier, len(offsets) + 4)

    def window_copy(part, target, slot):
        src, dst = (
            (hl.at[:, :, :, pl.ds(3 * LANES, LANES)], wl.at[:, :, :, pl.ds(LANES, LANES)]),
            (hl.at[:, :, :, pl.ds(2 * LANES, LANES)], wl.at[:, :, :, pl.ds(0, LANES)]),
            (hr.at[:, :, :, pl.ds(2 * LANES, 2 * LANES)], wr),
        )[part]
        return pltpu.make_async_remote_copy(
            src_ref=src, dst_ref=dst, send_sem=x_send.at[part, slot], recv_sem=x_recv.at[part],
            device_id={"mom": dev, "tm": target}, device_id_type=MESH,
        )

    def rim_copy(part):
        src, dst = ((hl, hlv), (hr, hrv))[part]
        return pltpu.make_async_remote_copy(
            src_ref=src.at[:, :, :, pl.ds(3 * LANES, LANES)],
            dst_ref=dst.at[:, :, :, pl.ds(0, LANES)],
            send_sem=x_send.at[3 + part, 0], recv_sem=x_recv.at[3 + part],
            device_id={"mom": dev, "tm": lax.rem(x + 1, TM)}, device_id_type=MESH,
        )

    @pl.when(x == TM - 1)
    def _():
        for part in range(3):
            for slot, target in enumerate((1, 0, 2)):
                window_copy(part, target, slot).start()

    @pl.when(x < TM - 1)
    def _():
        for part in range(2):
            rim_copy(part).start()

    @pl.when(x == 0)
    def _():
        zeros = jnp.zeros((2, HERE, ORB, LANES), F32)
        hlv[:, :, :, pl.ds(0, LANES)] = zeros
        hrv[:, :, :, pl.ds(0, LANES)] = zeros

    lane = lax.broadcasted_iota(jnp.int32, (1, LANES), 1)
    low_half = lane < HALF
    sign = jnp.where(low_half, -1.0, 1.0).astype(F32)

    coup_lane = jnp.zeros((1, LANES), F32)
    mf_lane = jnp.zeros((1, LANES), F32)
    for b in range(ORB):
        here = lax.rem(lane, ORB) == b
        coup_lane = jnp.where(here, coup[row * ORB + b], coup_lane)
        mf_lane = jnp.where(here, mf[row * ORB + b], mf_lane)
    strength = coup_lane * coup_lane
    newest = (lax.rem(lane, HALF) >= HALF - ORB) & (half == 1)
    mf_lane = jnp.where(newest, mf_lane, 0.0)
    first_row = lax.broadcasted_iota(jnp.int32, (KX * KY, 1), 0) == 0
    mf_term = jnp.where(first_row, mf_lane, 0.0)
    low_rows = lax.broadcasted_iota(jnp.int32, (1, 8, 1), 1) < 4

    def propagate(k, source, lanes_from, count):
        stack = jnp.concatenate([prop[0, k], prop[1, k]], axis=0)
        real = jnp.dot(
            stack, source[0, k, :, pl.ds(lanes_from, count)],
            precision=lax.Precision.HIGHEST, preferred_element_type=F32,
        )
        imag = jnp.dot(
            stack, source[1, k, :, pl.ds(lanes_from, count)],
            precision=lax.Precision.HIGHEST, preferred_element_type=F32,
        )
        return real[:ORB] - imag[ORB:], real[ORB:] + imag[:ORB]

    def build(k, slot, source_r, source_l, lanes_from):
        for lp, source in enumerate((source_r, source_l)):
            for c in range(2):
                first = source[c, k, :, pl.ds(lanes_from, LANES)]
                second = source[c, k, :, pl.ds(lanes_from + LANES, LANES)]
                for m in range(W):
                    shift = ORB * (m + 1)
                    if shift < LANES:
                        moved = pltpu.roll(
                            jnp.where(lane >= shift, first, second), LANES - shift, 1
                        )
                    else:
                        moved = second
                    high, low = split(moved * lag[m])
                    at = lp * LANES + m * ORB
                    hank[slot, 0, pl.ds(at, ORB), pl.ds(c * LANES, LANES)] = high
                    hank[slot, 1, pl.ds(at, ORB), pl.ds(c * LANES, LANES)] = low

    def send_window(p, k, real, imag):
        turned_real = pltpu.roll(real, HALF, 1)
        turned_imag = pltpu.roll(imag, HALF, 1)
        sendf[p, 0, pl.ds(k, ORB, stride=HERE), :] = jnp.where(low_half, real, turned_imag)
        sendf[p, 1, pl.ds(k, ORB, stride=HERE), :] = jnp.where(low_half, turned_real, imag)

    def forward_copy(p, target):
        return pltpu.make_async_remote_copy(
            src_ref=sendf.at[p, lax.rem(target, 2), pl.ds((target // 2) * HERE, HERE), :],
            dst_ref=fbuf.at[p, pl.ds((core * CHIPS + chip) * HERE, HERE), :],
            send_sem=f_send.at[p], recv_sem=f_recv.at[p],
            device_id={"mom": target * 2 + core, "tm": x}, device_id_type=MESH,
        )

    def back_copy(p, target):
        return pltpu.make_async_remote_copy(
            src_ref=sendb.at[p, target],
            dst_ref=rbuf.at[p, half, pl.ds(row * 8, 8), :],
            send_sem=b_send.at[p], recv_sem=b_recv.at[p],
            device_id={"mom": target * 2 + core, "tm": x}, device_id_type=MESH,
        )

    def pair_copy(p):
        block = fbuf.at[p, pl.ds(core * CHIPS * HERE, CHIPS * HERE), :]
        return pltpu.make_async_remote_copy(
            src_ref=block, dst_ref=block, send_sem=s_send.at[p], recv_sem=s_recv.at[p],
            device_id={"mom": chip * 2 + 1 - core, "tm": x}, device_id_type=MESH,
        )

    def arrived(p, k):
        columns = []
        for lp in range(2):
            first = rbuf[p, 0, pl.ds(lp * HERE + k, ORB, stride=8), :]
            second = rbuf[p, 1, pl.ds(lp * HERE + k, ORB, stride=8), :]
            real = jnp.where(low_half, first, pltpu.roll(second, HALF, 1))
            imag = jnp.where(low_half, pltpu.roll(first, HALF, 1), second)
            columns.append(jnp.concatenate([real, imag], axis=0))
        high, low = split(jnp.concatenate(columns, axis=1))
        return jnp.concatenate([high, low], axis=0)

    def collide(stack, slot):
        rows = 2 * ORB
        product = mm(stack, hank[slot, 0])
        total = product[:rows] + product[rows:] + mm(stack[:rows], hank[slot, 1])
        real = total[:ORB, :LANES] - total[ORB:, LANES:]
        imag = total[:ORB, LANES:] + total[ORB:, :LANES]
        return real, imag

    @pl.when(x == TM - 1)
    def _():
        for copy in own_window:
            copy.wait()

    @pl.when(x < TM - 1)
    def _():
        window_copy(0, 0, 0).wait_recv()

    for k in range(HERE):
        real, imag = propagate(k, wl, LANES, LANES)
        startw[0, k] = real
        startw[1, k] = imag
        send_window(0, k, real, imag)

    for p in range(PASSES):
        own = pltpu.make_async_copy(
            sendf.at[p, half, pl.ds(row * HERE, HERE), :],
            fbuf.at[p, pl.ds((core * CHIPS + chip) * HERE, HERE), :],
            f_own.at[p],
        )
        own.start()
        for dz, dy in offsets:
            forward_copy(p, peer_chip(dz, dy)).start()

        if p == 0:
            @pl.when(x < TM - 1)
            def _():
                window_copy(1, 0, 0).wait_recv()
                window_copy(2, 0, 0).wait_recv()

            for k in range(HERE):
                build(k, BLOCKS * HERE + k, wr, wl, 0)
            for load in loads:
                load.wait()

            @pl.when(x > 0)
            def _():
                for part in range(2):
                    rim_copy(part).wait_recv()
        else:
            for k in range(HERE):
                for block in (2 * (p - 1), 2 * (p - 1) + 1):
                    build(k, block * HERE + k, hrv, hlv, block * LANES)

        own.wait()
        landed = fbuf.at[p, pl.ds(0, (CHIPS - 1) * HERE), :]
        pltpu.make_async_copy(landed, landed, f_recv.at[p]).wait()
        pair_copy(p).start()
        pair_copy(p).wait_recv()

        here = fbuf[p]
        high, low = split(jnp.concatenate([here, pltpu.roll(here, HALF, 1) * sign], axis=0))
        both = mm(tab[0], jnp.concatenate([high, low], axis=1))
        pos = both[:, :LANES] + both[:, LANES:] + mm(tab[1], high)
        turned = pltpu.roll(pos, HALF, 1)
        square = pos * pos
        turned_square = pltpu.roll(square, HALF, 1)
        lesser = (strength * (square + turned_square) + mf_term) * pos
        pair = strength * jnp.where(low_half, square - turned_square, 2.0 * pos * turned)
        both = jnp.concatenate([lesser, pair], axis=1)
        other = jnp.concatenate(
            [pltpu.roll(lesser, HALF, 1) * -sign, pltpu.roll(pair, HALF, 1) * -sign], axis=1
        )
        high, low = split(jnp.concatenate([both, other], axis=0))
        mine = pl.ds(pl.multiple_of(core * (CHIPS * HERE), CHIPS * HERE), CHIPS * HERE)
        tab_high, tab_low = tab[0, mine, :], tab[1, mine, :]
        back = mm(tab_high, high) + mm(tab_high, low) + mm(tab_low, high)
        left = back[:, :LANES].reshape(CHIPS // 2, 8, LANES)
        right = back[:, LANES:].reshape(CHIPS // 2, 8, LANES)
        even = jnp.where(low_rows, left, pltpu.roll(right, 4, 1))
        odd = jnp.where(low_rows, pltpu.roll(left, 4, 1), right)
        for pair_index in range(CHIPS // 2):
            sendb[p, 2 * pair_index] = even[pair_index]
            sendb[p, 2 * pair_index + 1] = odd[pair_index]
        rbuf[p, half, pl.ds(pl.multiple_of(row * 8, 8), 8), :] = sendb[p, chip]
        for dz, dy in offsets:
            back_copy(p, peer_chip(dz, dy)).start()

        if p == 0:
            for k in range(HERE):
                real, imag = propagate(k, hlv, LANES, BLOCKS * LANES)
                startv[0, k] = real
                startv[1, k] = imag

        landed = sendb.at[p, pl.ds(0, CHIPS - 1)]
        pltpu.make_async_copy(landed, landed, b_recv.at[p]).wait()

        if p < PASSES - 1:
            for k in range(HERE):
                real, imag = collide(arrived(p, k), BLOCKS * HERE + k)
                send_window(p + 1, k, startw[0, k] + imag, startw[1, k] - real)
        else:
            for k in range(HERE):
                stack = arrived(p, k)
                for block in range(BLOCKS):
                    real, imag = collide(stack, block * HERE + k)
                    at = pl.ds(block * LANES, LANES)
                    out[0, k, :, at] = startv[0, k, :, at] + imag
                    out[1, k, :, at] = startv[1, k, :, at] - real

    for p in range(PASSES):
        sent = fbuf.at[p, pl.ds(0, (CHIPS - 1) * HERE), :]
        pltpu.make_async_copy(sent, sent, f_send.at[p]).wait()
        sent = sendb.at[p, pl.ds(0, CHIPS - 1)]
        pltpu.make_async_copy(sent, sent, b_send.at[p]).wait()
        pair_copy(p).wait_send()

    @pl.when(x == TM - 1)
    def _():
        for part in range(3):
            for slot in range(3):
                window_copy(part, slot, slot).wait_send()

    @pl.when(x < TM - 1)
    def _():
        for part in range(2):
            rim_copy(part).wait_send()


def on_device(table, hist_lesser, hist_retarded, propagator, coupling, mf_weight, lag_weight):
    vmem = pl.BlockSpec(memory_space=pltpu.VMEM)
    smem = pl.BlockSpec(memory_space=pltpu.SMEM)
    anywhere = pl.BlockSpec(memory_space=pl.ANY)
    padded = (2, HERE, ORB, (BLOCKS + 1) * LANES)
    return pl.pallas_call(
        kernel,
        out_shape=jax.ShapeDtypeStruct(hist_lesser.shape, F32),
        in_specs=[anywhere, anywhere, vmem, smem, smem, smem, anywhere],
        out_specs=vmem,
        scratch_shapes=[
            pltpu.VMEM(padded, F32),
            pltpu.VMEM(padded, F32),
            pltpu.VMEM((2, HERE, ORB, 2 * LANES), F32),
            pltpu.VMEM((2, HERE, ORB, 2 * LANES), F32),
            pltpu.VMEM((2, KX * KY, 2 * KX * KY), BF16),
            pltpu.VMEM((2, HERE, ORB, BLOCKS * LANES), F32),
            pltpu.VMEM((2, HERE, ORB, LANES), F32),
            pltpu.VMEM(((BLOCKS + 1) * HERE, 2, 2 * LANES, 2 * LANES), BF16),
            pltpu.VMEM((PASSES, 2, ORB * HERE, LANES), F32),
            pltpu.VMEM((PASSES, KX * KY, LANES), F32),
            pltpu.VMEM((PASSES, CHIPS, 8, LANES), F32),
            pltpu.VMEM((PASSES, 2, ORB * 8, LANES), F32),
            pltpu.SemaphoreType.DMA((5,)),
            pltpu.SemaphoreType.DMA((5, 3)),
            pltpu.SemaphoreType.DMA((5,)),
            pltpu.SemaphoreType.DMA((PASSES,)),
            pltpu.SemaphoreType.DMA((PASSES,)),
            pltpu.SemaphoreType.DMA((PASSES,)),
            pltpu.SemaphoreType.DMA((PASSES,)),
            pltpu.SemaphoreType.DMA((PASSES,)),
            pltpu.SemaphoreType.DMA((PASSES,)),
            pltpu.SemaphoreType.DMA((PASSES,)),
        ],
        compiler_params=pltpu.CompilerParams(
            collective_id=0, has_side_effects=True, vmem_limit_bytes=48 * 1024 * 1024
        ),
    )(hist_lesser, hist_retarded, propagator, coupling, mf_weight, lag_weight, table)


def solution(mesh):
    table = momentum_table()

    def step(*args):
        return jax.shard_map(
            on_device,
            mesh=mesh,
            in_specs=(
                P(None, None, None),
                P(None, "mom", None, "tm"),
                P(None, "mom", None, "tm"),
                P(None, "mom", None, None),
                P(),
                P(),
                P(),
            ),
            out_specs=P(None, "mom", None, "tm"),
            check_vma=False,
        )(jnp.asarray(table), *args)

    return step
```

```python
import functools
import math

import jax
import jax.numpy as jnp
import ml_dtypes
import numpy as np
from jax import lax
from jax.experimental import pallas as pl
from jax.experimental.pallas import tpu as pltpu
from jax.sharding import PartitionSpec as P

KX = 16
KY = 16
ORB = 16
W = 8
PASSES = 3
NZ, NY = 8, 4
CHIPS = NZ * NY
TM = 4
HERE = 4
LANES = W * ORB
HALF = LANES // 2
BLOCKS = 4

MESH = pl.DeviceIdType.MESH
F32 = jnp.float32
BF16 = jnp.bfloat16


def momentum_table():
    place = np.arange(KX * KY)
    core, chip, here = place // 128, place // 4 % 32, place % 4
    k = 8 * chip + 4 * core + here
    kx, ky = k // KY, k % KY
    turn = (kx[:, None] * kx[None, :]) % KX + (ky[:, None] * ky[None, :]) % KY
    phase = 2.0 * math.pi * turn / 16.0
    full = np.concatenate([np.cos(phase), np.sin(phase)], axis=1) / 16.0
    full = full.astype(np.float32)
    high = full.astype(ml_dtypes.bfloat16)
    low = (full - high.astype(np.float32)).astype(ml_dtypes.bfloat16)
    return np.stack([high, low])


def split(x):
    high = x.astype(BF16)
    return high, (x - high.astype(F32)).astype(BF16)


def mm(a, b):
    return jnp.dot(a, b, preferred_element_type=F32)


def kernel(
    hl, hr, prop_hbm, coup_hbm, mf_hbm, lag_hbm, table,
    out,
    prop, coup, mf, lag, hlv, hrv, wl, wr, tab, startv, startw, hank, sendf, fbuf, sendb, rbuf,
    load_sem, x_send, x_recv, f_send, f_recv, f_own, s_send, s_recv, b_send, b_recv,
):
    dev = lax.axis_index("mom")
    x = lax.axis_index("tm")
    core = lax.rem(dev, 2)
    chip = dev // 2
    z = chip // NY
    y = lax.rem(chip, NY)
    row = chip // 2
    half = lax.rem(chip, 2)

    def peer_chip(dz, dy):
        return lax.rem(z + dz, NZ) * NY + lax.rem(y + dy, NY)

    offsets = [(dz, dy) for dz in (4, 3, 5, 2, 6, 1, 7, 0) for dy in (2, 1, 3, 0) if dz or dy]

    barrier = pltpu.get_barrier_semaphore()
    for dx in (1, 2, 3):
        pl.semaphore_signal(
            barrier, inc=1, device_id={"mom": dev, "tm": lax.rem(x + dx, TM)}, device_id_type=MESH
        )
    for dz, dy in offsets:
        pl.semaphore_signal(
            barrier, inc=1, device_id={"mom": peer_chip(dz, dy) * 2 + core, "tm": x},
            device_id_type=MESH,
        )
    pl.semaphore_signal(
        barrier, inc=1, device_id={"mom": chip * 2 + 1 - core, "tm": x}, device_id_type=MESH
    )

    small = [
        pltpu.make_async_copy(source, place, load_sem.at[5 + slot])
        for slot, (source, place) in enumerate(
            ((prop_hbm, prop), (coup_hbm, coup), (mf_hbm, mf), (lag_hbm, lag))
        )
    ]
    for load in small:
        load.start()
    loads = [
        pltpu.make_async_copy(hl, hlv.at[:, :, :, pl.ds(LANES, BLOCKS * LANES)], load_sem.at[0]),
        pltpu.make_async_copy(hr, hrv.at[:, :, :, pl.ds(LANES, BLOCKS * LANES)], load_sem.at[1]),
        pltpu.make_async_copy(table, tab, load_sem.at[2]),
    ]
    for load in loads:
        load.start()

    own_window = [
        pltpu.make_async_copy(hl.at[:, :, :, pl.ds(2 * LANES, 2 * LANES)], wl, load_sem.at[3]),
        pltpu.make_async_copy(hr.at[:, :, :, pl.ds(2 * LANES, 2 * LANES)], wr, load_sem.at[4]),
    ]

    @pl.when(x == TM - 1)
    def _():
        for copy in own_window:
            copy.start()

    pl.semaphore_wait(barrier, len(offsets) + 4)

    def window_copy(part, target, slot):
        src, dst = (
            (hl.at[:, :, :, pl.ds(3 * LANES, LANES)], wl.at[:, :, :, pl.ds(LANES, LANES)]),
            (hl.at[:, :, :, pl.ds(2 * LANES, LANES)], wl.at[:, :, :, pl.ds(0, LANES)]),
            (hr.at[:, :, :, pl.ds(2 * LANES, 2 * LANES)], wr),
        )[part]
        return pltpu.make_async_remote_copy(
            src_ref=src, dst_ref=dst, send_sem=x_send.at[part, slot], recv_sem=x_recv.at[part],
            device_id={"mom": dev, "tm": target}, device_id_type=MESH,
        )

    def rim_copy(part):
        src, dst = ((hl, hlv), (hr, hrv))[part]
        return pltpu.make_async_remote_copy(
            src_ref=src.at[:, :, :, pl.ds(3 * LANES, LANES)],
            dst_ref=dst.at[:, :, :, pl.ds(0, LANES)],
            send_sem=x_send.at[3 + part, 0], recv_sem=x_recv.at[3 + part],
            device_id={"mom": dev, "tm": lax.rem(x + 1, TM)}, device_id_type=MESH,
        )

    @pl.when(x == TM - 1)
    def _():
        for part in range(3):
            for slot, target in enumerate((1, 0, 2)):
                window_copy(part, target, slot).start()

    @pl.when(x < TM - 1)
    def _():
        for part in range(2):
            rim_copy(part).start()

    @pl.when(x == 0)
    def _():
        zeros = jnp.zeros((2, HERE, ORB, LANES), F32)
        hlv[:, :, :, pl.ds(0, LANES)] = zeros
        hrv[:, :, :, pl.ds(0, LANES)] = zeros

    for load in small:
        load.wait()
    lane = lax.broadcasted_iota(jnp.int32, (1, LANES), 1)
    low_half = lane < HALF
    sign = jnp.where(low_half, -1.0, 1.0).astype(F32)

    coup_lane = jnp.zeros((1, LANES), F32)
    mf_lane = jnp.zeros((1, LANES), F32)
    for b in range(ORB):
        here = lax.rem(lane, ORB) == b
        coup_lane = jnp.where(here, coup[row * ORB + b], coup_lane)
        mf_lane = jnp.where(here, mf[row * ORB + b], mf_lane)
    strength = coup_lane * coup_lane
    newest = (lax.rem(lane, HALF) >= HALF - ORB) & (half == 1)
    mf_lane = jnp.where(newest, mf_lane, 0.0)
    first_row = lax.broadcasted_iota(jnp.int32, (KX * KY, 1), 0) == 0
    mf_term = jnp.where(first_row, mf_lane, 0.0)
    low_rows = lax.broadcasted_iota(jnp.int32, (1, 8, 1), 1) < 4

    def propagate(k, source, lanes_from, count):
        stack = jnp.concatenate([prop[0, k], prop[1, k]], axis=0)
        real = jnp.dot(
            stack, source[0, k, :, pl.ds(lanes_from, count)],
            precision=lax.Precision.HIGHEST, preferred_element_type=F32,
        )
        imag = jnp.dot(
            stack, source[1, k, :, pl.ds(lanes_from, count)],
            precision=lax.Precision.HIGHEST, preferred_element_type=F32,
        )
        return real[:ORB] - imag[ORB:], real[ORB:] + imag[:ORB]

    def build(k, slot, source_r, source_l, lanes_from):
        for lp, source in enumerate((source_r, source_l)):
            for c in range(2):
                first = source[c, k, :, pl.ds(lanes_from, LANES)]
                second = source[c, k, :, pl.ds(lanes_from + LANES, LANES)]
                for m in range(W):
                    shift = ORB * (m + 1)
                    if shift < LANES:
                        moved = pltpu.roll(
                            jnp.where(lane >= shift, first, second), LANES - shift, 1
                        )
                    else:
                        moved = second
                    high, low = split(moved * lag[m])
                    at = lp * LANES + m * ORB
                    hank[slot, 0, pl.ds(at, ORB), pl.ds(c * LANES, LANES)] = high
                    hank[slot, 1, pl.ds(at, ORB), pl.ds(c * LANES, LANES)] = low

    def send_window(p, k, real, imag):
        turned_real = pltpu.roll(real, HALF, 1)
        turned_imag = pltpu.roll(imag, HALF, 1)
        sendf[p, 0, pl.ds(k, ORB, stride=HERE), :] = jnp.where(low_half, real, turned_imag)
        sendf[p, 1, pl.ds(k, ORB, stride=HERE), :] = jnp.where(low_half, turned_real, imag)

    def forward_copy(p, target):
        return pltpu.make_async_remote_copy(
            src_ref=sendf.at[p, lax.rem(target, 2), pl.ds((target // 2) * HERE, HERE), :],
            dst_ref=fbuf.at[p, pl.ds((core * CHIPS + chip) * HERE, HERE), :],
            send_sem=f_send.at[p], recv_sem=f_recv.at[p],
            device_id={"mom": target * 2 + core, "tm": x}, device_id_type=MESH,
        )

    def back_copy(p, target):
        return pltpu.make_async_remote_copy(
            src_ref=sendb.at[p, target],
            dst_ref=rbuf.at[p, half, pl.ds(row * 8, 8), :],
            send_sem=b_send.at[p], recv_sem=b_recv.at[p],
            device_id={"mom": target * 2 + core, "tm": x}, device_id_type=MESH,
        )

    def pair_copy(p):
        block = fbuf.at[p, pl.ds(core * CHIPS * HERE, CHIPS * HERE), :]
        return pltpu.make_async_remote_copy(
            src_ref=block, dst_ref=block, send_sem=s_send.at[p], recv_sem=s_recv.at[p],
            device_id={"mom": chip * 2 + 1 - core, "tm": x}, device_id_type=MESH,
        )

    def arrived(p, k):
        columns = []
        for lp in range(2):
            first = rbuf[p, 0, pl.ds(lp * HERE + k, ORB, stride=8), :]
            second = rbuf[p, 1, pl.ds(lp * HERE + k, ORB, stride=8), :]
            real = jnp.where(low_half, first, pltpu.roll(second, HALF, 1))
            imag = jnp.where(low_half, pltpu.roll(first, HALF, 1), second)
            columns.append(jnp.concatenate([real, imag], axis=0))
        high, low = split(jnp.concatenate(columns, axis=1))
        return jnp.concatenate([high, low], axis=0)

    def collide(stack, slot):
        rows = 2 * ORB
        product = mm(stack, hank[slot, 0])
        total = product[:rows] + product[rows:] + mm(stack[:rows], hank[slot, 1])
        real = total[:ORB, :LANES] - total[ORB:, LANES:]
        imag = total[:ORB, LANES:] + total[ORB:, :LANES]
        return real, imag

    @pl.when(x == TM - 1)
    def _():
        for copy in own_window:
            copy.wait()

    @pl.when(x < TM - 1)
    def _():
        window_copy(0, 0, 0).wait_recv()

    for k in range(HERE):
        real, imag = propagate(k, wl, LANES, LANES)
        startw[0, k] = real
        startw[1, k] = imag
        send_window(0, k, real, imag)

    for p in range(PASSES):
        own = pltpu.make_async_copy(
            sendf.at[p, half, pl.ds(row * HERE, HERE), :],
            fbuf.at[p, pl.ds((core * CHIPS + chip) * HERE, HERE), :],
            f_own.at[p],
        )
        own.start()
        for dz, dy in offsets:
            forward_copy(p, peer_chip(dz, dy)).start()

        if p == 0:
            @pl.when(x < TM - 1)
            def _():
                window_copy(1, 0, 0).wait_recv()
                window_copy(2, 0, 0).wait_recv()

            for k in range(HERE):
                build(k, BLOCKS * HERE + k, wr, wl, 0)
            for load in loads:
                load.wait()

            @pl.when(x > 0)
            def _():
                for part in range(2):
                    rim_copy(part).wait_recv()
        else:
            for k in range(HERE):
                for block in (2 * (p - 1), 2 * (p - 1) + 1):
                    build(k, block * HERE + k, hrv, hlv, block * LANES)

        own.wait()
        landed = fbuf.at[p, pl.ds(0, (CHIPS - 1) * HERE), :]
        pltpu.make_async_copy(landed, landed, f_recv.at[p]).wait()
        pair_copy(p).start()
        pair_copy(p).wait_recv()

        here = fbuf[p]
        high, low = split(jnp.concatenate([here, pltpu.roll(here, HALF, 1) * sign], axis=0))
        both = mm(tab[0], jnp.concatenate([high, low], axis=1))
        pos = both[:, :LANES] + both[:, LANES:] + mm(tab[1], high)
        turned = pltpu.roll(pos, HALF, 1)
        square = pos * pos
        turned_square = pltpu.roll(square, HALF, 1)
        lesser = (strength * (square + turned_square) + mf_term) * pos
        pair = strength * jnp.where(low_half, square - turned_square, 2.0 * pos * turned)
        both = jnp.concatenate([lesser, pair], axis=1)
        other = jnp.concatenate(
            [pltpu.roll(lesser, HALF, 1) * -sign, pltpu.roll(pair, HALF, 1) * -sign], axis=1
        )
        high, low = split(jnp.concatenate([both, other], axis=0))
        mine = pl.ds(pl.multiple_of(core * (CHIPS * HERE), CHIPS * HERE), CHIPS * HERE)
        tab_high, tab_low = tab[0, mine, :], tab[1, mine, :]
        back = mm(tab_high, high) + mm(tab_high, low) + mm(tab_low, high)
        left = back[:, :LANES].reshape(CHIPS // 2, 8, LANES)
        right = back[:, LANES:].reshape(CHIPS // 2, 8, LANES)
        even = jnp.where(low_rows, left, pltpu.roll(right, 4, 1))
        odd = jnp.where(low_rows, pltpu.roll(left, 4, 1), right)
        for pair_index in range(CHIPS // 2):
            sendb[p, 2 * pair_index] = even[pair_index]
            sendb[p, 2 * pair_index + 1] = odd[pair_index]
        rbuf[p, half, pl.ds(pl.multiple_of(row * 8, 8), 8), :] = sendb[p, chip]
        for dz, dy in offsets:
            back_copy(p, peer_chip(dz, dy)).start()

        if p == 0:
            for k in range(HERE):
                real, imag = propagate(k, hlv, LANES, BLOCKS * LANES)
                startv[0, k] = real
                startv[1, k] = imag

        landed = sendb.at[p, pl.ds(0, CHIPS - 1)]
        pltpu.make_async_copy(landed, landed, b_recv.at[p]).wait()

        if p < PASSES - 1:
            for k in range(HERE):
                real, imag = collide(arrived(p, k), BLOCKS * HERE + k)
                send_window(p + 1, k, startw[0, k] + imag, startw[1, k] - real)
        else:
            for k in range(HERE):
                stack = arrived(p, k)
                for block in range(BLOCKS):
                    real, imag = collide(stack, block * HERE + k)
                    at = pl.ds(block * LANES, LANES)
                    out[0, k, :, at] = startv[0, k, :, at] + imag
                    out[1, k, :, at] = startv[1, k, :, at] - real

    for p in range(PASSES):
        sent = fbuf.at[p, pl.ds(0, (CHIPS - 1) * HERE), :]
        pltpu.make_async_copy(sent, sent, f_send.at[p]).wait()
        sent = sendb.at[p, pl.ds(0, CHIPS - 1)]
        pltpu.make_async_copy(sent, sent, b_send.at[p]).wait()
        pair_copy(p).wait_send()

    @pl.when(x == TM - 1)
    def _():
        for part in range(3):
            for slot in range(3):
                window_copy(part, slot, slot).wait_send()

    @pl.when(x < TM - 1)
    def _():
        for part in range(2):
            rim_copy(part).wait_send()


def on_device(table, hist_lesser, hist_retarded, propagator, coupling, mf_weight, lag_weight):
    vmem = pl.BlockSpec(memory_space=pltpu.VMEM)
    hbm = pl.BlockSpec(memory_space=pltpu.HBM)
    padded = (2, HERE, ORB, (BLOCKS + 1) * LANES)
    return pl.pallas_call(
        kernel,
        out_shape=jax.ShapeDtypeStruct(hist_lesser.shape, F32),
        in_specs=[hbm] * 7,
        out_specs=vmem,
        scratch_shapes=[
            pltpu.VMEM((2, HERE, ORB, ORB), F32),
            pltpu.SMEM((ORB * ORB,), F32),
            pltpu.SMEM((ORB * ORB,), F32),
            pltpu.SMEM((W,), F32),
            pltpu.VMEM(padded, F32),
            pltpu.VMEM(padded, F32),
            pltpu.VMEM((2, HERE, ORB, 2 * LANES), F32),
            pltpu.VMEM((2, HERE, ORB, 2 * LANES), F32),
            pltpu.VMEM((2, KX * KY, 2 * KX * KY), BF16),
            pltpu.VMEM((2, HERE, ORB, BLOCKS * LANES), F32),
            pltpu.VMEM((2, HERE, ORB, LANES), F32),
            pltpu.VMEM(((BLOCKS + 1) * HERE, 2, 2 * LANES, 2 * LANES), BF16),
            pltpu.VMEM((PASSES, 2, ORB * HERE, LANES), F32),
            pltpu.VMEM((PASSES, KX * KY, LANES), F32),
            pltpu.VMEM((PASSES, CHIPS, 8, LANES), F32),
            pltpu.VMEM((PASSES, 2, ORB * 8, LANES), F32),
            pltpu.SemaphoreType.DMA((9,)),
            pltpu.SemaphoreType.DMA((5, 3)),
            pltpu.SemaphoreType.DMA((5,)),
            pltpu.SemaphoreType.DMA((PASSES,)),
            pltpu.SemaphoreType.DMA((PASSES,)),
            pltpu.SemaphoreType.DMA((PASSES,)),
            pltpu.SemaphoreType.DMA((PASSES,)),
            pltpu.SemaphoreType.DMA((PASSES,)),
            pltpu.SemaphoreType.DMA((PASSES,)),
            pltpu.SemaphoreType.DMA((PASSES,)),
        ],
        compiler_params=pltpu.CompilerParams(
            collective_id=0, has_side_effects=True, vmem_limit_bytes=67043328
        ),
    )(hist_lesser, hist_retarded, propagator, coupling, mf_weight, lag_weight, table)


def solution(mesh):
    table = momentum_table()

    def step(*args):
        return jax.shard_map(
            on_device,
            mesh=mesh,
            in_specs=(
                P(None, None, None),
                P(None, "mom", None, "tm"),
                P(None, "mom", None, "tm"),
                P(None, "mom", None, None),
                P(),
                P(),
                P(),
            ),
            out_specs=P(None, "mom", None, "tm"),
            check_vma=False,
        )(jnp.asarray(table), *args)

    return step
```

```python
import math

import jax
import jax.numpy as jnp
import ml_dtypes
import numpy as np
from jax import lax
from jax.experimental import pallas as pl
from jax.experimental.pallas import tpu as pltpu
from jax.sharding import PartitionSpec as P

KX = 16
KY = 16
K = KX * KY
ORB = 16
W = 8
PASSES = 3
NZ, NY = 8, 4
CHIPS = NZ * NY
CORES = 2
TM = 4
HERE = 4
LANES = W * ORB
QUARTER = LANES // 4
HALF = LANES // 2
BLOCKS = 4

MESH = pl.DeviceIdType.MESH
F32 = jnp.float32
BF16 = jnp.bfloat16


def halves(full):
    full = full.astype(np.float32)
    high = full.astype(ml_dtypes.bfloat16)
    low = (full - high.astype(np.float32)).astype(ml_dtypes.bfloat16)
    return np.stack([high, low])


def momentum_tables():
    place = np.arange(K)

    def number(core, chip, here):
        return 8 * chip + 4 * core + here

    plain = number(place // 128, place // 4 % 32, place % 4)
    parted = number(place // 64 % 2, place // 2 % 32, place % 2 + 2 * (place // 128))

    def table(rows, columns):
        turn = (rows[:, None] // KY) * (columns[None, :] // KY) % KX
        turn = turn + (rows[:, None] % KY) * (columns[None, :] % KY) % KY
        phase = 2.0 * math.pi * turn / 16.0
        return halves(np.concatenate([np.cos(phase), np.sin(phase)], axis=1) / 16.0)

    return np.stack([table(plain, parted), table(plain, plain)])


def split(x):
    high = x.astype(BF16)
    return high, (x - high.astype(F32)).astype(BF16)


def mm(a, b):
    return jnp.dot(a, b, preferred_element_type=F32)


def ring(step, size):
    return min(step % size, -step % size)


def offsets(limit):
    found = [(dz, dy) for dz in range(NZ) for dy in range(NY) if ring(dz, NZ) + ring(dy, NY) <= limit]
    return sorted(found, key=lambda o: -(ring(o[0], NZ) + ring(o[1], NY)))


def kernel(
    hl, hr, prop_hbm, coup_hbm, mf_hbm, lag_hbm, tables,
    out,
    prop, propw, coup, mf, lag, hlv, hrv, wl, wr, tabs, startv, startw, hank, sendf, fbuf, sendb, rbuf,
    load_sem, x_send, x_recv, f_send, f_recv, f_own, b_send, b_recv,
):
    dev = lax.axis_index("mom")
    x = lax.axis_index("tm")
    core = lax.rem(dev, CORES)
    chip = dev // CORES
    z = chip // NY
    y = lax.rem(chip, NY)
    mate = x + 1 - 2 * lax.rem(x, 2)
    odd = lax.rem(x, 2)

    def place(dz, dy):
        return lax.rem(z + dz, NZ), lax.rem(y + dy, NY)

    def label_of(zz, yy, plane_odd):
        shift = 1 - plane_odd
        return lax.rem(zz + (NZ // 2) * shift, NZ) * NY + lax.rem(yy + (NY // 2) * shift, NY)

    def device(zz, yy, cc, plane):
        return {"mom": (zz * NY + yy) * CORES + cc, "tm": plane}

    def each(limit, plane, plane_odd, own):
        for dz, dy in offsets(limit):
            zz, yy = place(dz, dy)
            for flip in (1, 0):
                if own and not (dz or dy or flip):
                    continue
                cc = 1 - core if flip else core
                yield zz, yy, cc, plane, plane_odd

    label = label_of(z, y, odd)
    row = label // 2
    quarter = lax.rem(label, 2) * 2 + core
    slot_here = core * CHIPS + label
    far = NZ + NY

    def near(limit_own, limit_mate):
        yield from each(limit_mate, mate, 1 - odd, False)
        yield from each(limit_own, x, odd, True)

    barrier = pltpu.get_barrier_semaphore()

    def greet(targets):
        for zz, yy, cc, plane, _ in targets:
            pl.semaphore_signal(barrier, inc=1, device_id=device(zz, yy, cc, plane), device_id_type=MESH)

    @pl.when(x == 3)
    def _():
        greet(near(far, 2))

    @pl.when(x == 2)
    def _():
        greet(near(3, far))
        greet([(z, y, core, 1, 1)])

    @pl.when(x < 2)
    def _():
        greet(each(3, 3 - x, 1 - odd, False))
        greet(each(2, 2 + x, odd, False))
        greet(near(3, 2))

    small = [
        pltpu.make_async_copy(source, target, load_sem.at[4 + number])
        for number, (source, target) in enumerate(
            ((prop_hbm, prop), (coup_hbm, coup), (mf_hbm, mf), (lag_hbm, lag))
        )
    ]
    own_window = [
        pltpu.make_async_copy(hl.at[:, :, :, pl.ds(2 * LANES, 2 * LANES)], wl, load_sem.at[8]),
        pltpu.make_async_copy(hr.at[:, :, :, pl.ds(2 * LANES, 2 * LANES)], wr, load_sem.at[9]),
        pltpu.make_async_copy(prop_hbm, propw, load_sem.at[10]),
    ]
    loads = [
        pltpu.make_async_copy(hl, hlv.at[:, :, :, pl.ds(LANES, BLOCKS * LANES)], load_sem.at[0]),
        pltpu.make_async_copy(hr, hrv.at[:, :, :, pl.ds(LANES, BLOCKS * LANES)], load_sem.at[1]),
    ]
    tables_in = pltpu.make_async_copy(tables, tabs, load_sem.at[2])

    @pl.when(x == 3)
    def _():
        for copy in own_window:
            copy.start()

    for load in small + loads:
        load.start()
    tables_in.start()
    for load in small:
        load.wait()

    lane = lax.broadcasted_iota(jnp.int32, (1, LANES), 1)
    low_half = lane < HALF
    block_of_lane = lane // QUARTER
    first_of_two = lax.rem(block_of_lane, 2) == 0
    sign = jnp.where(first_of_two, -1.0, 1.0).astype(F32)

    coup_lane = jnp.zeros((1, LANES), F32)
    mf_lane = jnp.zeros((1, LANES), F32)
    for b in range(ORB):
        here = lax.rem(lane, ORB) == b
        coup_lane = jnp.where(here, coup[row * ORB + b], coup_lane)
        mf_lane = jnp.where(here, mf[row * ORB + b], mf_lane)
    strength = coup_lane * coup_lane
    newest = (lax.rem(lane, QUARTER) >= QUARTER - ORB) & (quarter == 3)
    mf_lane = jnp.where(newest, mf_lane, 0.0)
    first_row = lax.broadcasted_iota(jnp.int32, (K, 1), 0) == 0
    mf_term = jnp.where(first_row, mf_lane, 0.0)

    def turn(value):
        return jnp.where(
            first_of_two, pltpu.roll(value, LANES - QUARTER, 1), pltpu.roll(value, QUARTER, 1)
        )

    def transpose_blocks(parts):
        result = []
        for j in range(4):
            total = parts[j]
            for i in range(4):
                if i == j:
                    continue
                moved = pltpu.roll(parts[i], (QUARTER * (i - j)) % LANES, 1)
                total = jnp.where(block_of_lane == i, moved, total)
            result.append(total)
        return result

    def propagate(step, k, source, lanes_from, count):
        stack = jnp.concatenate([step[0, k], step[1, k]], axis=0)
        real, imag = (
            jnp.dot(
                stack, source[c, k, :, pl.ds(lanes_from, count)],
                precision=lax.Precision.HIGHEST, preferred_element_type=F32,
            )
            for c in range(2)
        )
        return real[:ORB] - imag[ORB:], real[ORB:] + imag[:ORB]

    def build(k, slot, source_r, source_l, lanes_from):
        for lp, source in enumerate((source_r, source_l)):
            for c in range(2):
                first = source[c, k, :, pl.ds(lanes_from, LANES)]
                second = source[c, k, :, pl.ds(lanes_from + LANES, LANES)]
                for m in range(W):
                    shift = ORB * (m + 1)
                    if shift < LANES:
                        moved = pltpu.roll(jnp.where(lane >= shift, first, second), LANES - shift, 1)
                    else:
                        moved = second
                    high, low = split(moved * lag[m])
                    at = lp * LANES + m * ORB
                    hank[slot, 0, pl.ds(at, ORB), pl.ds(c * LANES, LANES)] = high
                    hank[slot, 1, pl.ds(at, ORB), pl.ds(c * LANES, LANES)] = low

    def build_blocks(blocks):
        @pl.loop(0, HERE)
        def _(k):
            for block in blocks:
                build(k, block * HERE + k, hrv, hlv, block * LANES)

    def pack_window(p, reals, imags):
        for r in range(2):
            parts = transpose_blocks([reals[r], imags[r], reals[r + 2], imags[r + 2]])
            for w in range(4):
                sendf[p, w, pl.ds(r, ORB, stride=2), :] = parts[w]

    def forward_copy(p, target):
        zz, yy, cc, plane, plane_odd = target
        goal = label_of(zz, yy, plane_odd)
        return pltpu.make_async_remote_copy(
            src_ref=sendf.at[p, lax.rem(goal, 2) * 2 + cc, pl.ds((goal // 2) * 2, 2), :],
            dst_ref=fbuf.at[p, pl.ds(slot_here * 2, 2), :],
            send_sem=f_send.at[p], recv_sem=f_recv.at[p],
            device_id=device(zz, yy, cc, plane), device_id_type=MESH,
        )

    def own_forward(p):
        return pltpu.make_async_copy(
            sendf.at[p, quarter, pl.ds(row * 2, 2), :],
            fbuf.at[p, pl.ds(slot_here * 2, 2), :],
            f_own.at[p],
        )

    def goal_slot(p, zz, yy, cc, plane_odd):
        goal = label_of(zz, yy, plane_odd) if p < PASSES - 1 else zz * NY + yy
        return cc * CHIPS + goal

    def back_copy(p, target):
        zz, yy, cc, plane, plane_odd = target
        return pltpu.make_async_remote_copy(
            src_ref=sendb.at[p, pl.ds(goal_slot(p, zz, yy, cc, plane_odd) * HERE, HERE), :],
            dst_ref=rbuf.at[p, quarter, pl.ds(row * HERE, HERE), :],
            send_sem=b_send.at[p], recv_sem=b_recv.at[p],
            device_id=device(zz, yy, cc, plane), device_id_type=MESH,
        )

    def own_back(p):
        return pltpu.make_async_copy(
            sendb.at[p, pl.ds(goal_slot(p, z, y, core, odd) * HERE, HERE), :],
            rbuf.at[p, quarter, pl.ds(row * HERE, HERE), :],
            f_own.at[PASSES + p],
        )

    def wait_rows(rows, sem):
        some = sendb.at[0, pl.ds(0, rows), :]
        pltpu.make_async_copy(some, some, sem).wait()

    others = CHIPS * CORES - 1

    def real_space(p):
        here = fbuf[p]
        both = jnp.concatenate([here, turn(here) * sign], axis=0)
        high = both.astype(BF16).astype(F32)
        low = both - high
        front = jnp.where(low_half, high, pltpu.roll(low, HALF, 1)).astype(BF16)
        rear = jnp.where(low_half, pltpu.roll(high, HALF, 1), low).astype(BF16)
        count = K // 2
        stack = jnp.concatenate([front[:count], rear[:count], front[count:], rear[count:]], axis=0)
        main = mm(tabs[0, 0], stack)
        rest = mm(tabs[0, 1], stack)
        pos = main + pltpu.roll(main, HALF, 1) + jnp.where(low_half, rest, pltpu.roll(rest, HALF, 1))
        turned = turn(pos)
        square = pos * pos
        turned_square = turned * turned
        lesser = (strength * (square + turned_square) + mf_term) * pos
        pair = strength * jnp.where(first_of_two, square - turned_square, 2.0 * pos * turned)
        both = jnp.where(low_half, lesser, pair)
        high, low = split(jnp.concatenate([both, turn(both) * -sign], axis=0))
        main = mm(tabs[1, 0], jnp.concatenate([high, low], axis=1))
        sendb[p] = main[:, :LANES] + main[:, LANES:] + mm(tabs[1, 1], high)

    def send_back(p):
        own_back(p).start()
        for target in near(3, 2):
            back_copy(p, target).start()

    def wait_back(p):
        own_back(p).wait()
        wait_rows(others * HERE, b_recv.at[p])

    def arrived(p, k):
        parts = transpose_blocks([rbuf[p, w, pl.ds(k, ORB, stride=HERE), :] for w in range(4)])
        lesser_real, lesser_imag, pair_real, pair_imag = parts
        high, low = split(
            jnp.concatenate(
                [
                    jnp.concatenate([lesser_real, pair_real], axis=1),
                    jnp.concatenate([lesser_imag, pair_imag], axis=1),
                ],
                axis=0,
            )
        )
        return jnp.concatenate([high, low], axis=0)

    def collide(stack, slot):
        rows = 2 * ORB
        product = mm(stack, hank[slot, 0])
        total = product[:rows] + product[rows:] + mm(stack[:rows], hank[slot, 1])
        real = total[:ORB, :LANES] - total[ORB:, LANES:]
        imag = total[:ORB, LANES:] + total[ORB:, :LANES]
        return real, imag

    def start_window():
        reals, imags = [], []
        for k in range(HERE):
            real, imag = propagate(propw, k, wl, LANES, LANES)
            startw[0, k] = real
            startw[1, k] = imag
            reals.append(real)
            imags.append(imag)
        return reals, imags

    def window_copy(part):
        src, dst = ((hr.at[:, :, :, pl.ds(2 * LANES, 2 * LANES)], wr),
                    (hl.at[:, :, :, pl.ds(2 * LANES, 2 * LANES)], wl),
                    (prop_hbm, propw))[part]
        zz, yy = place(NZ // 2, NY // 2)
        return pltpu.make_async_remote_copy(
            src_ref=src, dst_ref=dst, send_sem=x_send.at[part], recv_sem=x_recv.at[part],
            device_id=device(zz, yy, core, 2), device_id_type=MESH,
        )

    def rim_copy(part):
        src, dst = ((hl, hlv), (hr, hrv))[part]
        return pltpu.make_async_remote_copy(
            src_ref=src.at[:, :, :, pl.ds((BLOCKS - 1) * LANES, LANES)],
            dst_ref=dst.at[:, :, :, pl.ds(0, LANES)],
            send_sem=x_send.at[3 + part], recv_sem=x_recv.at[3 + part],
            device_id=device(z, y, core, lax.rem(x + 1, TM)), device_id_type=MESH,
        )

    @pl.when(x == 3)
    def _():
        for copy in own_window:
            copy.wait()
        pack_window(0, *start_window())
        own_forward(0).start()
        pl.semaphore_wait(barrier, others + 2 * (others + 1))
        for target in each(far, 2, 0, False):
            forward_copy(0, target).start()
        for target in each(far, 3, 1, True):
            forward_copy(0, target).start()
        for part in range(3):
            window_copy(part).start()

    @pl.when(x == 2)
    def _():
        pl.semaphore_wait(barrier, others + others + 1)

    @pl.when(x == 1)
    def _():
        pl.semaphore_wait(barrier, others + 1)

    @pl.when(x == 0)
    def _():
        pl.semaphore_wait(barrier, others)

    @pl.when(x < TM - 1)
    def _():
        for part in range(2):
            rim_copy(part).start()

    @pl.when(x == 0)
    def _():
        zeros = jnp.zeros((2, HERE, ORB, LANES), F32)
        hlv[:, :, :, pl.ds(0, LANES)] = zeros
        hrv[:, :, :, pl.ds(0, LANES)] = zeros

    for load in loads:
        load.wait()

    def start_all():
        @pl.loop(0, HERE)
        def _(k):
            real, imag = propagate(prop, k, hlv, LANES, BLOCKS * LANES)
            startv[0, k] = real
            startv[1, k] = imag

    start_all()
    build_blocks((1, 2, 3))
    tables_in.wait()

    @pl.when(x >= 2)
    def _():
        for p in range(PASSES - 1):
            if p == 0:
                @pl.when(x == 3)
                def _():
                    own_forward(0).wait()
                    wait_rows(others * 2, f_recv.at[0])

                @pl.when(x == 2)
                def _():
                    wait_rows((others + 1) * 2, f_recv.at[0])
            else:
                own_forward(p).wait()
                wait_rows(others * 2, f_recv.at[p])
            real_space(p)
            send_back(p)
            if p == 0:
                @pl.when(x == 2)
                def _():
                    for part in range(3):
                        window_copy(part).wait_recv()
                    start_window()

                @pl.loop(0, HERE)
                def _(k):
                    build(k, BLOCKS * HERE + k, wr, wl, 0)

            wait_back(p)
            reals, imags = [], []
            for k in range(HERE):
                real, imag = collide(arrived(p, k), BLOCKS * HERE + k)
                reals.append(startw[0, k] + imag)
                imags.append(startw[1, k] - real)
            pack_window(p + 1, reals, imags)
            own_forward(p + 1).start()
            if p + 1 == PASSES - 1:
                for target in each(3, 3 - x, 1 - odd, False):
                    forward_copy(p + 1, target).start()
                for target in each(2, x - 2, odd, False):
                    forward_copy(p + 1, target).start()
            for target in near(3, 2):
                forward_copy(p + 1, target).start()

    @pl.when(x > 0)
    def _():
        for part in range(2):
            rim_copy(part).wait_recv()

    build_blocks((0,))

    p = PASSES - 1

    @pl.when(x >= 2)
    def _():
        own_forward(p).wait()
        wait_rows(others * 2, f_recv.at[p])

    @pl.when(x < 2)
    def _():
        wait_rows((others + 1) * 2, f_recv.at[p])

    real_space(p)
    send_back(p)
    wait_back(p)
    for k in range(HERE):
        stack = arrived(p, k)
        for block in range(BLOCKS):
            real, imag = collide(stack, block * HERE + k)
            at = pl.ds(block * LANES, LANES)
            out[0, k, :, at] = startv[0, k, :, at] + imag
            out[1, k, :, at] = startv[1, k, :, at] - real

    wait_rows(others * HERE, b_send.at[p])

    @pl.when(x >= 2)
    def _():
        wait_rows(others * HERE, b_send.at[0])
        wait_rows(others * HERE, b_send.at[1])
        wait_rows(others * 2, f_send.at[1])
        wait_rows((2 * others + 1) * 2, f_send.at[2])

    @pl.when(x == 3)
    def _():
        wait_rows((2 * others + 1) * 2, f_send.at[0])
        for part in range(3):
            window_copy(part).wait_send()

    @pl.when(x < TM - 1)
    def _():
        for part in range(2):
            rim_copy(part).wait_send()


def on_device(tables, hist_lesser, hist_retarded, propagator, coupling, mf_weight, lag_weight):
    vmem = pl.BlockSpec(memory_space=pltpu.VMEM)
    hbm = pl.BlockSpec(memory_space=pltpu.HBM)
    padded = (2, HERE, ORB, (BLOCKS + 1) * LANES)
    return pl.pallas_call(
        kernel,
        out_shape=jax.ShapeDtypeStruct(hist_lesser.shape, F32),
        in_specs=[hbm] * 7,
        out_specs=vmem,
        scratch_shapes=[
            pltpu.VMEM((2, HERE, ORB, ORB), F32),
            pltpu.VMEM((2, HERE, ORB, ORB), F32),
            pltpu.SMEM((ORB * ORB,), F32),
            pltpu.SMEM((ORB * ORB,), F32),
            pltpu.SMEM((W,), F32),
            pltpu.VMEM(padded, F32),
            pltpu.VMEM(padded, F32),
            pltpu.VMEM((2, HERE, ORB, 2 * LANES), F32),
            pltpu.VMEM((2, HERE, ORB, 2 * LANES), F32),
            pltpu.VMEM((2, 2, K, 2 * K), BF16),
            pltpu.VMEM((2, HERE, ORB, BLOCKS * LANES), F32),
            pltpu.VMEM((2, HERE, ORB, LANES), F32),
            pltpu.VMEM(((BLOCKS + 1) * HERE, 2, 2 * LANES, 2 * LANES), BF16),
            pltpu.VMEM((PASSES, 4, 2 * ORB, LANES), F32),
            pltpu.VMEM((PASSES, K // 2, LANES), F32),
            pltpu.VMEM((PASSES, K, LANES), F32),
            pltpu.VMEM((PASSES, 4, HERE * ORB, LANES), F32),
            pltpu.SemaphoreType.DMA((11,)),
            pltpu.SemaphoreType.DMA((5,)),
            pltpu.SemaphoreType.DMA((5,)),
            pltpu.SemaphoreType.DMA((PASSES,)),
            pltpu.SemaphoreType.DMA((PASSES,)),
            pltpu.SemaphoreType.DMA((2 * PASSES,)),
            pltpu.SemaphoreType.DMA((PASSES,)),
            pltpu.SemaphoreType.DMA((PASSES,)),
        ],
        compiler_params=pltpu.CompilerParams(
            collective_id=0, has_side_effects=True, vmem_limit_bytes=67043328
        ),
    )(hist_lesser, hist_retarded, propagator, coupling, mf_weight, lag_weight, tables)


def solution(mesh):
    tables = momentum_tables()

    def step(*args):
        return jax.shard_map(
            on_device,
            mesh=mesh,
            in_specs=(
                P(None, None, None, None),
                P(None, "mom", None, "tm"),
                P(None, "mom", None, "tm"),
                P(None, "mom", None, None),
                P(),
                P(),
                P(),
            ),
            out_specs=P(None, "mom", None, "tm"),
            check_vma=False,
        )(jnp.asarray(tables), *args)

    return step
```

```python
import math

import jax
import jax.numpy as jnp
import ml_dtypes
import numpy as np
from jax import lax
from jax.experimental import pallas as pl
from jax.experimental.pallas import tpu as pltpu
from jax.sharding import PartitionSpec as P

KX = 16
KY = 16
ORB = 16
W = 8
PASSES = 3
NZ, NY = 8, 4
CHIPS = NZ * NY
TM = 4
HERE = 4
LANES = W * ORB
HALF = LANES // 2
BLOCKS = 4

MESH = pl.DeviceIdType.MESH
F32 = jnp.float32
BF16 = jnp.bfloat16


def momentum_tables():
    place = np.arange(KX * KY)
    core, chip, here = place // 128, place // 4 % 32, place % 4
    k = 8 * chip + 4 * core + here
    kx, ky = k // KY, k % KY
    turn = (kx[:, None] * kx[None, :]) % KX + (ky[:, None] * ky[None, :]) % KY
    phase = 2.0 * math.pi * turn / 16.0
    full = np.stack([np.cos(phase), np.sin(phase)]).astype(np.float32) / 16.0
    high = full.astype(ml_dtypes.bfloat16)
    low = (full - high.astype(np.float32)).astype(ml_dtypes.bfloat16)
    both = np.stack([high, low])
    ahead = both.reshape(2, 2, 256, 2, 128).transpose(3, 0, 2, 1, 4).reshape(2, 2, 256, 256)
    back = both.reshape(2, 2, 2, 128, 256).transpose(2, 0, 3, 1, 4).reshape(2, 2, 128, 512)
    return ahead, back


def split(x):
    high = x.astype(BF16)
    return high, (x - high.astype(F32)).astype(BF16)


def mm(a, b):
    return jnp.dot(a, b, preferred_element_type=F32)


def ring(step, size):
    return min(step % size, -step % size)


OFFSETS = sorted(
    ((dz, dy) for dz in range(NZ) for dy in range(NY)), key=lambda o: -(ring(o[0], NZ) + ring(o[1], NY))
)


def kernel(
    hl, hr, prop_hbm, coup_hbm, mf_hbm, lag_hbm, ahead_hbm, back_hbm,
    out,
    prop, coup, mf, lag, hlv, hrv, ahead, backward, startv, hank, sendf, fbuf, sendb, rbuf,
    load_sem, x_send, x_recv, f_send, f_recv, f_own, s_send, s_recv, b_send, b_recv,
):
    dev = lax.axis_index("mom")
    x = lax.axis_index("tm")
    core = lax.rem(dev, 2)
    chip = dev // 2
    z = chip // NY
    y = lax.rem(chip, NY)
    row = chip // 2
    half = lax.rem(chip, 2)

    def peer_chip(dz, dy):
        return lax.rem(z + dz, NZ) * NY + lax.rem(y + dy, NY)

    others = CHIPS - 1
    last = TM - 1

    barrier = pltpu.get_barrier_semaphore()

    def greet(target, plane):
        pl.semaphore_signal(
            barrier, inc=1, device_id={"mom": target, "tm": plane}, device_id_type=MESH
        )

    @pl.when(x < last)
    def _():
        for dz, dy in OFFSETS:
            greet(peer_chip(dz, dy) * 2 + core, last)

    for dz, dy in OFFSETS[:-1]:
        greet(peer_chip(dz, dy) * 2 + core, x)
    greet(chip * 2 + 1 - core, x)

    @pl.when(x > 0)
    def _():
        greet(dev, x - 1)

    small = [
        pltpu.make_async_copy(source, place, load_sem.at[4 + slot])
        for slot, (source, place) in enumerate(
            ((prop_hbm, prop), (coup_hbm, coup), (mf_hbm, mf), (lag_hbm, lag))
        )
    ]
    for load in small:
        load.start()
    loads = [
        pltpu.make_async_copy(hl, hlv.at[:, :, :, pl.ds(LANES, BLOCKS * LANES)], load_sem.at[0]),
        pltpu.make_async_copy(hr, hrv.at[:, :, :, pl.ds(LANES, BLOCKS * LANES)], load_sem.at[1]),
        pltpu.make_async_copy(ahead_hbm, ahead, load_sem.at[2]),
        pltpu.make_async_copy(back_hbm.at[core], backward, load_sem.at[3]),
    ]
    for load in loads:
        load.start()

    def rim_copy(part):
        src, dst = ((hl, hlv), (hr, hrv))[part]
        return pltpu.make_async_remote_copy(
            src_ref=src.at[:, :, :, pl.ds(3 * LANES, LANES)],
            dst_ref=dst.at[:, :, :, pl.ds(0, LANES)],
            send_sem=x_send.at[part], recv_sem=x_recv.at[part],
            device_id={"mom": dev, "tm": lax.rem(x + 1, TM)}, device_id_type=MESH,
        )

    for load in small:
        load.wait()
    lane = lax.broadcasted_iota(jnp.int32, (1, LANES), 1)
    low_half = lane < HALF
    sign = jnp.where(low_half, -1.0, 1.0).astype(F32)

    coup_lane = jnp.zeros((1, LANES), F32)
    mf_lane = jnp.zeros((1, LANES), F32)
    for b in range(ORB):
        here = lax.rem(lane, ORB) == b
        coup_lane = jnp.where(here, coup[row * ORB + b], coup_lane)
        mf_lane = jnp.where(here, mf[row * ORB + b], mf_lane)
    strength = coup_lane * coup_lane
    newest = (lax.rem(lane, HALF) >= HALF - ORB) & (half == 1)
    mf_lane = jnp.where(newest, mf_lane, 0.0)
    first_row = lax.broadcasted_iota(jnp.int32, (KX * KY, 1), 0) == 0
    mf_term = jnp.where(first_row, mf_lane, 0.0)
    low_rows = lax.broadcasted_iota(jnp.int32, (1, 8, 1), 1) < 4

    def propagate(k, source, lanes_from, count):
        stack = jnp.concatenate([prop[0, k], prop[1, k]], axis=0)
        real = jnp.dot(
            stack, source[0, k, :, pl.ds(lanes_from, count)],
            precision=lax.Precision.HIGHEST, preferred_element_type=F32,
        )
        imag = jnp.dot(
            stack, source[1, k, :, pl.ds(lanes_from, count)],
            precision=lax.Precision.HIGHEST, preferred_element_type=F32,
        )
        return real[:ORB] - imag[ORB:], real[ORB:] + imag[:ORB]

    def build(k, slot, source_r, source_l, lanes_from):
        for lp, source in enumerate((source_r, source_l)):
            for c in range(2):
                first = source[c, k, :, pl.ds(lanes_from, LANES)]
                second = source[c, k, :, pl.ds(lanes_from + LANES, LANES)]
                for m in range(W):
                    shift = ORB * (m + 1)
                    if shift < LANES:
                        moved = pltpu.roll(
                            jnp.where(lane >= shift, first, second), LANES - shift, 1
                        )
                    else:
                        moved = second
                    high, low = split(moved * lag[m])
                    at = lp * LANES + m * ORB
                    hank[slot, 0, pl.ds(at, ORB), pl.ds(c * LANES, LANES)] = high
                    hank[slot, 1, pl.ds(at, ORB), pl.ds(c * LANES, LANES)] = low

    def send_window(p, k, real, imag):
        turned_real = pltpu.roll(real, HALF, 1)
        turned_imag = pltpu.roll(imag, HALF, 1)
        sendf[p, 0, pl.ds(k, ORB, stride=HERE), :] = jnp.where(low_half, real, turned_imag)
        sendf[p, 1, pl.ds(k, ORB, stride=HERE), :] = jnp.where(low_half, turned_real, imag)

    def forward_copy(p, target, plane):
        return pltpu.make_async_remote_copy(
            src_ref=sendf.at[p, lax.rem(target, 2), pl.ds((target // 2) * HERE, HERE), :],
            dst_ref=fbuf.at[p, pl.ds((core * CHIPS + chip) * HERE, HERE), :],
            send_sem=f_send.at[p], recv_sem=f_recv.at[p],
            device_id={"mom": target * 2 + core, "tm": plane}, device_id_type=MESH,
        )

    def back_copy(p, target):
        return pltpu.make_async_remote_copy(
            src_ref=sendb.at[p, target],
            dst_ref=rbuf.at[p, half, pl.ds(row * 8, 8), :],
            send_sem=b_send.at[p], recv_sem=b_recv.at[p],
            device_id={"mom": target * 2 + core, "tm": x}, device_id_type=MESH,
        )

    def pair_copy(p):
        block = fbuf.at[p, pl.ds(core * CHIPS * HERE, CHIPS * HERE), :]
        return pltpu.make_async_remote_copy(
            src_ref=block, dst_ref=block, send_sem=s_send.at[p], recv_sem=s_recv.at[p],
            device_id={"mom": chip * 2 + 1 - core, "tm": x}, device_id_type=MESH,
        )

    def arrived(p, k):
        columns = []
        for lp in range(2):
            first = rbuf[p, 0, pl.ds(lp * HERE + k, ORB, stride=8), :]
            second = rbuf[p, 1, pl.ds(lp * HERE + k, ORB, stride=8), :]
            real = jnp.where(low_half, first, pltpu.roll(second, HALF, 1))
            imag = jnp.where(low_half, pltpu.roll(first, HALF, 1), second)
            columns.append(jnp.concatenate([real, imag], axis=0))
        high, low = split(jnp.concatenate(columns, axis=1))
        return jnp.concatenate([high, low], axis=0)

    def collide(stack, slot):
        rows = 2 * ORB
        product = mm(stack, hank[slot, 0])
        total = product[:rows] + product[rows:] + mm(stack[:rows], hank[slot, 1])
        real = total[:ORB, :LANES] - total[ORB:, LANES:]
        imag = total[:ORB, LANES:] + total[ORB:, :LANES]
        return real, imag

    def own_forward(p):
        return pltpu.make_async_copy(
            sendf.at[p, half, pl.ds(row * HERE, HERE), :],
            fbuf.at[p, pl.ds((core * CHIPS + chip) * HERE, HERE), :],
            f_own.at[p],
        )

    def send_forward(p):
        own_forward(p).start()
        for dz, dy in OFFSETS:
            target = peer_chip(dz, dy)
            if p == PASSES - 1:
                for plane in (1, 0, 2):
                    forward_copy(p, target, plane).start()
            if dz or dy:
                forward_copy(p, target, last).start()

    def wait_forward(p):
        own_forward(p).wait()
        wait_rows(others * HERE, f_recv.at[p])

    def wait_rows(rows, sem):
        while rows:
            some = fbuf.at[0, pl.ds(0, min(rows, KX * KY)), :]
            pltpu.make_async_copy(some, some, sem).wait()
            rows -= min(rows, KX * KY)

    def start_block(block):
        for k in range(HERE):
            real, imag = propagate(k, hlv, (block + 1) * LANES, LANES)
            at = pl.ds(block * LANES, LANES)
            startv[0, k, :, at] = real
            startv[1, k, :, at] = imag

    def build_blocks(blocks):
        @pl.loop(0, HERE)
        def _(k):
            for block in blocks:
                build(k, block * HERE + k, hrv, hlv, block * LANES)

    def ahead_part(p, which):
        here = fbuf[p, pl.ds(pl.multiple_of(which * (CHIPS * HERE), CHIPS * HERE), CHIPS * HERE), :]
        high, low = split(jnp.concatenate([here, pltpu.roll(here, HALF, 1) * sign], axis=0))
        both = mm(ahead[which, 0], jnp.concatenate([high, low], axis=1))
        return both[:, :LANES] + both[:, LANES:] + mm(ahead[which, 1], high)

    def real_space(p):
        pair_copy(p).start()
        pos = ahead_part(p, core)
        pair_copy(p).wait_recv()
        pos = pos + ahead_part(p, 1 - core)
        turned = pltpu.roll(pos, HALF, 1)
        square = pos * pos
        turned_square = pltpu.roll(square, HALF, 1)
        lesser = (strength * (square + turned_square) + mf_term) * pos
        pair = strength * jnp.where(low_half, square - turned_square, 2.0 * pos * turned)
        both = jnp.concatenate([lesser, pair], axis=1)
        other = jnp.concatenate(
            [pltpu.roll(lesser, HALF, 1) * -sign, pltpu.roll(pair, HALF, 1) * -sign], axis=1
        )
        high, low = split(jnp.concatenate([both, other], axis=0))
        back = mm(backward[0], high) + mm(backward[0], low) + mm(backward[1], high)
        left = back[:, :LANES].reshape(CHIPS // 2, 8, LANES)
        right = back[:, LANES:].reshape(CHIPS // 2, 8, LANES)
        even = jnp.where(low_rows, left, pltpu.roll(right, 4, 1))
        odd = jnp.where(low_rows, pltpu.roll(left, 4, 1), right)
        for pair_index in range(CHIPS // 2):
            sendb[p, 2 * pair_index] = even[pair_index]
            sendb[p, 2 * pair_index + 1] = odd[pair_index]
        for dz, dy in OFFSETS[:-1]:
            back_copy(p, peer_chip(dz, dy)).start()
        rbuf[p, half, pl.ds(pl.multiple_of(row * 8, 8), 8), :] = sendb[p, chip]

    def wait_back(p):
        landed = sendb.at[p, pl.ds(0, others)]
        pltpu.make_async_copy(landed, landed, b_recv.at[p]).wait()

    for load in loads:
        load.wait()
    start_block(BLOCKS - 1)

    @pl.when(x == last)
    def _():
        newest_times = pl.ds((BLOCKS - 1) * LANES, LANES)
        for k in range(HERE):
            send_window(0, k, startv[0, k, :, newest_times], startv[1, k, :, newest_times])
        pl.semaphore_wait(barrier, others + 1 + (TM - 1) * CHIPS)
        send_forward(0)

    @pl.when(x < last)
    def _():
        pl.semaphore_wait(barrier, others + 2)
        for part in range(2):
            rim_copy(part).start()

    @pl.when(x == 0)
    def _():
        zeros = jnp.zeros((2, HERE, ORB, LANES), F32)
        hlv[:, :, :, pl.ds(0, LANES)] = zeros
        hrv[:, :, :, pl.ds(0, LANES)] = zeros

    build_blocks((BLOCKS - 1,))
    for block in range(BLOCKS - 1):
        start_block(block)

    @pl.when(x == last)
    def _():
        for p in range(PASSES - 1):
            if p:
                build_blocks((2,))
            wait_forward(p)
            real_space(p)
            if p == 0:
                build_blocks((1,))
            wait_back(p)
            for k in range(HERE):
                real, imag = collide(arrived(p, k), (BLOCKS - 1) * HERE + k)
                at = pl.ds((BLOCKS - 1) * LANES, LANES)
                send_window(p + 1, k, startv[0, k, :, at] + imag, startv[1, k, :, at] - real)
            send_forward(p + 1)

    @pl.when(x < last)
    def _():
        build_blocks((1, 2))

    @pl.when(x > 0)
    def _():
        for part in range(2):
            rim_copy(part).wait_recv()

    build_blocks((0,))

    p = PASSES - 1

    @pl.when(x == last)
    def _():
        wait_forward(p)

    @pl.when(x < last)
    def _():
        wait_rows(CHIPS * HERE, f_recv.at[p])

    real_space(p)
    wait_back(p)
    for k in range(HERE):
        stack = arrived(p, k)
        for block in range(BLOCKS):
            real, imag = collide(stack, block * HERE + k)
            at = pl.ds(block * LANES, LANES)
            out[0, k, :, at] = startv[0, k, :, at] + imag
            out[1, k, :, at] = startv[1, k, :, at] - real

    def sent_back(p):
        sent = sendb.at[p, pl.ds(0, others)]
        pltpu.make_async_copy(sent, sent, b_send.at[p]).wait()
        pair_copy(p).wait_send()

    sent_back(p)

    @pl.when(x == last)
    def _():
        for p in range(PASSES):
            wait_rows((others if p < PASSES - 1 else others + (TM - 1) * CHIPS) * HERE, f_send.at[p])
            if p < PASSES - 1:
                sent_back(p)

    @pl.when(x < last)
    def _():
        for part in range(2):
            rim_copy(part).wait_send()


def on_device(ahead, back, hist_lesser, hist_retarded, propagator, coupling, mf_weight, lag_weight):
    vmem = pl.BlockSpec(memory_space=pltpu.VMEM)
    hbm = pl.BlockSpec(memory_space=pltpu.HBM)
    padded = (2, HERE, ORB, (BLOCKS + 1) * LANES)
    return pl.pallas_call(
        kernel,
        out_shape=pltpu.VMEM(hist_lesser.shape, F32),
        in_specs=[hbm] * 8,
        out_specs=vmem,
        scratch_shapes=[
            pltpu.VMEM((2, HERE, ORB, ORB), F32),
            pltpu.SMEM((ORB * ORB,), F32),
            pltpu.SMEM((ORB * ORB,), F32),
            pltpu.SMEM((W,), F32),
            pltpu.VMEM(padded, F32),
            pltpu.VMEM(padded, F32),
            pltpu.VMEM((2, 2, KX * KY, KX * KY), BF16),
            pltpu.VMEM((2, CHIPS * HERE, 2 * KX * KY), BF16),
            pltpu.VMEM((2, HERE, ORB, BLOCKS * LANES), F32),
            pltpu.VMEM((BLOCKS * HERE, 2, 2 * LANES, 2 * LANES), BF16),
            pltpu.VMEM((PASSES, 2, ORB * HERE, LANES), F32),
            pltpu.VMEM((PASSES, KX * KY, LANES), F32),
            pltpu.VMEM((PASSES, CHIPS, 8, LANES), F32),
            pltpu.VMEM((PASSES, 2, ORB * 8, LANES), F32),
            pltpu.SemaphoreType.DMA((8,)),
            pltpu.SemaphoreType.DMA((2,)),
            pltpu.SemaphoreType.DMA((2,)),
            pltpu.SemaphoreType.DMA((PASSES,)),
            pltpu.SemaphoreType.DMA((PASSES,)),
            pltpu.SemaphoreType.DMA((PASSES,)),
            pltpu.SemaphoreType.DMA((PASSES,)),
            pltpu.SemaphoreType.DMA((PASSES,)),
            pltpu.SemaphoreType.DMA((PASSES,)),
            pltpu.SemaphoreType.DMA((PASSES,)),
        ],
        compiler_params=pltpu.CompilerParams(
            collective_id=0, has_side_effects=True, vmem_limit_bytes=67043328 - 4 * math.prod(hist_lesser.shape)
        ),
    )(hist_lesser, hist_retarded, propagator, coupling, mf_weight, lag_weight, ahead, back)


def solution(mesh):
    tables = momentum_tables()

    def step(*args):
        return jax.shard_map(
            on_device,
            mesh=mesh,
            in_specs=(
                P(None, None, None, None),
                P(None, None, None, None),
                P(None, "mom", None, "tm"),
                P(None, "mom", None, "tm"),
                P(None, "mom", None, None),
                P(),
                P(),
                P(),
            ),
            out_specs=P(None, "mom", None, "tm"),
            check_vma=False,
        )(*map(jnp.asarray, tables), *args)

    return step
```

```python
import math

import jax
import jax.numpy as jnp
import ml_dtypes
import numpy as np
from jax import lax
from jax.experimental import pallas as pl
from jax.experimental.pallas import tpu as pltpu
from jax.sharding import PartitionSpec as P

KX = 16
KY = 16
K = KX * KY
ORB = 16
W = 8
PASSES = 3
NZ, NY = 8, 4
CHIPS = NZ * NY
CORES = 2
TM = 4
HERE = 4
LANES = W * ORB
QUARTER = LANES // 4
HALF = LANES // 2
BLOCKS = 4

MESH = pl.DeviceIdType.MESH
F32 = jnp.float32
BF16 = jnp.bfloat16


def halves(full):
    full = full.astype(np.float32)
    high = full.astype(ml_dtypes.bfloat16)
    low = (full - high.astype(np.float32)).astype(ml_dtypes.bfloat16)
    return np.stack([high, low])


def momentum_tables():
    place = np.arange(K)

    def number(core, chip, here):
        return 8 * chip + 4 * core + here

    plain = number(place // 128, place // 4 % 32, place % 4)
    parted = number(place // 64 % 2, place // 2 % 32, place % 2 + 2 * (place // 128))

    def table(rows, columns):
        turn = (rows[:, None] // KY) * (columns[None, :] // KY) % KX
        turn = turn + (rows[:, None] % KY) * (columns[None, :] % KY) % KY
        phase = 2.0 * math.pi * turn / 16.0
        return halves(np.concatenate([np.cos(phase), np.sin(phase)], axis=1) / 16.0)

    return np.stack([table(plain, parted), table(plain, plain)])


def split(x):
    high = x.astype(BF16)
    return high, (x - high.astype(F32)).astype(BF16)


def mm(a, b):
    return jnp.dot(a, b, preferred_element_type=F32)


def ring(step, size):
    return min(step % size, -step % size)


PLACES = [
    (dz, dy, flip)
    for dz, dy in sorted(
        ((dz, dy) for dz in range(NZ) for dy in range(NY)), key=lambda o: -(ring(o[0], NZ) + ring(o[1], NY))
    )
    for flip in (1, 0)
]


def kernel(
    hl, hr, prop_hbm, coup_hbm, mf_hbm, lag_hbm, tables,
    out,
    prop, coup, mf, lag, hlv, hrv, tabs, startv, hank, sendf, fbuf, sendb, rbuf,
    load_sem, x_send, x_recv, f_send, f_recv, f_own, b_send, b_recv,
):
    dev = lax.axis_index("mom")
    x = lax.axis_index("tm")
    core = lax.rem(dev, CORES)
    chip = dev // CORES
    z = chip // NY
    y = lax.rem(chip, NY)
    last = TM - 1
    others = CHIPS * CORES - 1
    row = chip // 2
    quarter = lax.rem(chip, 2) * 2 + core
    slot_here = core * CHIPS + chip

    def at_place(place):
        dz, dy, flip = place
        return lax.rem(z + dz, NZ) * NY + lax.rem(y + dy, NY), 1 - core if flip else core

    def device(goal, cc, plane):
        return {"mom": goal * CORES + cc, "tm": plane}

    barrier = pltpu.get_barrier_semaphore()

    def greet(goal, cc, plane):
        pl.semaphore_signal(barrier, inc=1, device_id=device(goal, cc, plane), device_id_type=MESH)

    @pl.when(x < last)
    def _():
        for place in PLACES:
            greet(*at_place(place), last)

    for place in PLACES[:-1]:
        greet(*at_place(place), x)

    @pl.when(x > 0)
    def _():
        greet(chip, core, x - 1)

    small = [
        pltpu.make_async_copy(source, target, load_sem.at[4 + number])
        for number, (source, target) in enumerate(
            ((prop_hbm, prop), (coup_hbm, coup), (mf_hbm, mf), (lag_hbm, lag))
        )
    ]
    loads = [
        pltpu.make_async_copy(hl, hlv.at[:, :, :, pl.ds(LANES, BLOCKS * LANES)], load_sem.at[0]),
        pltpu.make_async_copy(hr, hrv.at[:, :, :, pl.ds(LANES, BLOCKS * LANES)], load_sem.at[1]),
    ]
    tables_in = pltpu.make_async_copy(tables, tabs, load_sem.at[2])

    for load in small + loads:
        load.start()
    tables_in.start()
    for load in small:
        load.wait()

    lane = lax.broadcasted_iota(jnp.int32, (1, LANES), 1)
    low_half = lane < HALF
    block_of_lane = lane // QUARTER
    first_of_two = lax.rem(block_of_lane, 2) == 0
    sign = jnp.where(first_of_two, -1.0, 1.0).astype(F32)

    coup_lane = jnp.zeros((1, LANES), F32)
    mf_lane = jnp.zeros((1, LANES), F32)
    for b in range(ORB):
        here = lax.rem(lane, ORB) == b
        coup_lane = jnp.where(here, coup[row * ORB + b], coup_lane)
        mf_lane = jnp.where(here, mf[row * ORB + b], mf_lane)
    strength = coup_lane * coup_lane
    newest = (lax.rem(lane, QUARTER) >= QUARTER - ORB) & (quarter == 3)
    mf_lane = jnp.where(newest, mf_lane, 0.0)
    first_row = lax.broadcasted_iota(jnp.int32, (K, 1), 0) == 0
    mf_term = jnp.where(first_row, mf_lane, 0.0)

    def turn(value):
        return jnp.where(
            first_of_two, pltpu.roll(value, LANES - QUARTER, 1), pltpu.roll(value, QUARTER, 1)
        )

    def transpose_blocks(parts):
        result = []
        for j in range(4):
            total = parts[j]
            for i in range(4):
                if i == j:
                    continue
                moved = pltpu.roll(parts[i], (QUARTER * (i - j)) % LANES, 1)
                total = jnp.where(block_of_lane == i, moved, total)
            result.append(total)
        return result

    def start_block(block):
        at = pl.ds(block * LANES, LANES)
        for k in range(HERE):
            stack = jnp.concatenate([prop[0, k], prop[1, k]], axis=0)
            real, imag = (
                jnp.dot(
                    stack, hlv[c, k, :, pl.ds((block + 1) * LANES, LANES)],
                    precision=lax.Precision.HIGHEST, preferred_element_type=F32,
                )
                for c in range(2)
            )
            startv[0, k, :, at] = real[:ORB] - imag[ORB:]
            startv[1, k, :, at] = real[ORB:] + imag[:ORB]

    def build(k, slot, source_r, source_l, lanes_from):
        for lp, source in enumerate((source_r, source_l)):
            for c in range(2):
                first = source[c, k, :, pl.ds(lanes_from, LANES)]
                second = source[c, k, :, pl.ds(lanes_from + LANES, LANES)]
                for m in range(W):
                    shift = ORB * (m + 1)
                    if shift < LANES:
                        moved = pltpu.roll(jnp.where(lane >= shift, first, second), LANES - shift, 1)
                    else:
                        moved = second
                    high, low = split(moved * lag[m])
                    at = lp * LANES + m * ORB
                    hank[slot, 0, pl.ds(at, ORB), pl.ds(c * LANES, LANES)] = high
                    hank[slot, 1, pl.ds(at, ORB), pl.ds(c * LANES, LANES)] = low

    def build_blocks(blocks):
        @pl.loop(0, HERE)
        def _(k):
            for block in blocks:
                build(k, block * HERE + k, hrv, hlv, block * LANES)

    def pack_window(p, reals, imags):
        for r in range(2):
            parts = transpose_blocks([reals[r], imags[r], reals[r + 2], imags[r + 2]])
            for w in range(4):
                sendf[p, w, pl.ds(r, ORB, stride=2), :] = parts[w]

    def forward_copy(p, place, plane):
        goal, cc = at_place(place)
        return pltpu.make_async_remote_copy(
            src_ref=sendf.at[p, lax.rem(goal, 2) * 2 + cc, pl.ds((goal // 2) * 2, 2), :],
            dst_ref=fbuf.at[p, pl.ds(slot_here * 2, 2), :],
            send_sem=f_send.at[p], recv_sem=f_recv.at[p],
            device_id=device(goal, cc, plane), device_id_type=MESH,
        )

    def own_forward(p):
        return pltpu.make_async_copy(
            sendf.at[p, quarter, pl.ds(row * 2, 2), :],
            fbuf.at[p, pl.ds(slot_here * 2, 2), :],
            f_own.at[p],
        )

    def back_copy(p, place):
        goal, cc = at_place(place)
        return pltpu.make_async_remote_copy(
            src_ref=sendb.at[p, pl.ds((cc * CHIPS + goal) * HERE, HERE), :],
            dst_ref=rbuf.at[p, quarter, pl.ds(row * HERE, HERE), :],
            send_sem=b_send.at[p], recv_sem=b_recv.at[p],
            device_id=device(goal, cc, x), device_id_type=MESH,
        )

    def own_back(p):
        return pltpu.make_async_copy(
            sendb.at[p, pl.ds(slot_here * HERE, HERE), :],
            rbuf.at[p, quarter, pl.ds(row * HERE, HERE), :],
            f_own.at[PASSES + p],
        )

    def wait_rows(rows, sem):
        while rows:
            some = sendb.at[0, pl.ds(0, min(rows, K)), :]
            pltpu.make_async_copy(some, some, sem).wait()
            rows -= min(rows, K)

    def send_forward(p):
        if p == PASSES - 1:
            for plane in range(last):
                for place in PLACES:
                    forward_copy(p, place, plane).start()
        own_forward(p).start()
        for place in PLACES[:-1]:
            forward_copy(p, place, last).start()

    def wait_forward(p):
        own_forward(p).wait()
        wait_rows(others * 2, f_recv.at[p])

    def real_space(p):
        here = fbuf[p]
        both = jnp.concatenate([here, turn(here) * sign], axis=0)
        high = both.astype(BF16).astype(F32)
        low = both - high
        front = jnp.where(low_half, high, pltpu.roll(low, HALF, 1)).astype(BF16)
        rear = jnp.where(low_half, pltpu.roll(high, HALF, 1), low).astype(BF16)
        count = K // 2
        stack = jnp.concatenate([front[:count], rear[:count], front[count:], rear[count:]], axis=0)
        main = mm(tabs[0, 0], stack)
        rest = mm(tabs[0, 1], stack)
        pos = main + pltpu.roll(main, HALF, 1) + jnp.where(low_half, rest, pltpu.roll(rest, HALF, 1))
        turned = turn(pos)
        square = pos * pos
        turned_square = turned * turned
        lesser = (strength * (square + turned_square) + mf_term) * pos
        pair = strength * jnp.where(first_of_two, square - turned_square, 2.0 * pos * turned)
        both = jnp.where(low_half, lesser, pair)
        high, low = split(jnp.concatenate([both, turn(both) * -sign], axis=0))
        main = mm(tabs[1, 0], jnp.concatenate([high, low], axis=1))
        sendb[p] = main[:, :LANES] + main[:, LANES:] + mm(tabs[1, 1], high)

    def send_back(p):
        own_back(p).start()
        for place in PLACES[:-1]:
            back_copy(p, place).start()

    def wait_back(p):
        own_back(p).wait()
        wait_rows(others * HERE, b_recv.at[p])

    def arrived(p, k):
        parts = transpose_blocks([rbuf[p, w, pl.ds(k, ORB, stride=HERE), :] for w in range(4)])
        lesser_real, lesser_imag, pair_real, pair_imag = parts
        high, low = split(
            jnp.concatenate(
                [
                    jnp.concatenate([lesser_real, pair_real], axis=1),
                    jnp.concatenate([lesser_imag, pair_imag], axis=1),
                ],
                axis=0,
            )
        )
        return jnp.concatenate([high, low], axis=0)

    def collide(stack, slot):
        rows = 2 * ORB
        product = mm(stack, hank[slot, 0])
        total = product[:rows] + product[rows:] + mm(stack[:rows], hank[slot, 1])
        real = total[:ORB, :LANES] - total[ORB:, LANES:]
        imag = total[:ORB, LANES:] + total[ORB:, :LANES]
        return real, imag

    def rim_copy(part):
        src, dst = ((hl, hlv), (hr, hrv))[part]
        return pltpu.make_async_remote_copy(
            src_ref=src.at[:, :, :, pl.ds((BLOCKS - 1) * LANES, LANES)],
            dst_ref=dst.at[:, :, :, pl.ds(0, LANES)],
            send_sem=x_send.at[part], recv_sem=x_recv.at[part],
            device_id=device(chip, core, lax.rem(x + 1, TM)), device_id_type=MESH,
        )

    for load in loads:
        load.wait()
    start_block(BLOCKS - 1)
    newest_times = pl.ds((BLOCKS - 1) * LANES, LANES)

    @pl.when(x == last)
    def _():
        pack_window(0, *([startv[c, k, :, newest_times] for k in range(HERE)] for c in range(2)))
        pl.semaphore_wait(barrier, others + last * (others + 1))
        send_forward(0)

    @pl.when(x < last)
    def _():
        pl.semaphore_wait(barrier, others + 1)
        for part in range(2):
            rim_copy(part).start()

    @pl.when(x == 0)
    def _():
        zeros = jnp.zeros((2, HERE, ORB, LANES), F32)
        hlv[:, :, :, pl.ds(0, LANES)] = zeros
        hrv[:, :, :, pl.ds(0, LANES)] = zeros

    build_blocks((BLOCKS - 1,))
    for block in range(BLOCKS - 1):
        start_block(block)
    tables_in.wait()

    @pl.when(x == last)
    def _():
        for p in range(PASSES - 1):
            if p:
                build_blocks((2,))
            wait_forward(p)
            real_space(p)
            send_back(p)
            if p == 0:
                build_blocks((1,))
            wait_back(p)
            reals, imags = [], []
            for k in range(HERE):
                real, imag = collide(arrived(p, k), (BLOCKS - 1) * HERE + k)
                reals.append(startv[0, k, :, newest_times] + imag)
                imags.append(startv[1, k, :, newest_times] - real)
            pack_window(p + 1, reals, imags)
            send_forward(p + 1)

    @pl.when(x < last)
    def _():
        build_blocks((1, 2))

    @pl.when(x > 0)
    def _():
        for part in range(2):
            rim_copy(part).wait_recv()

    build_blocks((0,))

    p = PASSES - 1

    @pl.when(x == last)
    def _():
        wait_forward(p)

    @pl.when(x < last)
    def _():
        wait_rows((others + 1) * 2, f_recv.at[p])

    real_space(p)
    send_back(p)
    wait_back(p)
    for k in range(HERE):
        stack = arrived(p, k)
        for block in range(BLOCKS):
            real, imag = collide(stack, block * HERE + k)
            at = pl.ds(block * LANES, LANES)
            out[0, k, :, at] = startv[0, k, :, at] + imag
            out[1, k, :, at] = startv[1, k, :, at] - real

    wait_rows(others * HERE, b_send.at[p])

    @pl.when(x == last)
    def _():
        for p in range(PASSES - 1):
            wait_rows(others * HERE, b_send.at[p])
            wait_rows(others * 2, f_send.at[p])
        wait_rows((others + last * (others + 1)) * 2, f_send.at[PASSES - 1])

    @pl.when(x < last)
    def _():
        for part in range(2):
            rim_copy(part).wait_send()


def on_device(tables, hist_lesser, hist_retarded, propagator, coupling, mf_weight, lag_weight):
    vmem = pl.BlockSpec(memory_space=pltpu.VMEM)
    hbm = pl.BlockSpec(memory_space=pltpu.HBM)
    padded = (2, HERE, ORB, (BLOCKS + 1) * LANES)
    return pl.pallas_call(
        kernel,
        out_shape=pltpu.VMEM(hist_lesser.shape, F32),
        in_specs=[hbm] * 7,
        out_specs=vmem,
        scratch_shapes=[
            pltpu.VMEM((2, HERE, ORB, ORB), F32),
            pltpu.SMEM((ORB * ORB,), F32),
            pltpu.SMEM((ORB * ORB,), F32),
            pltpu.SMEM((W,), F32),
            pltpu.VMEM(padded, F32),
            pltpu.VMEM(padded, F32),
            pltpu.VMEM((2, 2, K, 2 * K), BF16),
            pltpu.VMEM((2, HERE, ORB, BLOCKS * LANES), F32),
            pltpu.VMEM((BLOCKS * HERE, 2, 2 * LANES, 2 * LANES), BF16),
            pltpu.VMEM((PASSES, 4, 2 * ORB, LANES), F32),
            pltpu.VMEM((PASSES, K // 2, LANES), F32),
            pltpu.VMEM((PASSES, K, LANES), F32),
            pltpu.VMEM((PASSES, 4, HERE * ORB, LANES), F32),
            pltpu.SemaphoreType.DMA((8,)),
            pltpu.SemaphoreType.DMA((2,)),
            pltpu.SemaphoreType.DMA((2,)),
            pltpu.SemaphoreType.DMA((PASSES,)),
            pltpu.SemaphoreType.DMA((PASSES,)),
            pltpu.SemaphoreType.DMA((2 * PASSES,)),
            pltpu.SemaphoreType.DMA((PASSES,)),
            pltpu.SemaphoreType.DMA((PASSES,)),
        ],
        compiler_params=pltpu.CompilerParams(
            collective_id=0, has_side_effects=True, vmem_limit_bytes=67043328 - 4 * math.prod(hist_lesser.shape)
        ),
    )(hist_lesser, hist_retarded, propagator, coupling, mf_weight, lag_weight, tables)


def solution(mesh):
    tables = momentum_tables()

    def step(*args):
        return jax.shard_map(
            on_device,
            mesh=mesh,
            in_specs=(
                P(None, None, None, None),
                P(None, "mom", None, "tm"),
                P(None, "mom", None, "tm"),
                P(None, "mom", None, None),
                P(),
                P(),
                P(),
            ),
            out_specs=P(None, "mom", None, "tm"),
            check_vma=False,
        )(jnp.asarray(tables), *args)

    return step
```

```python
import math

import jax
import jax.numpy as jnp
import ml_dtypes
import numpy as np
from jax import lax
from jax.experimental import pallas as pl
from jax.experimental.pallas import tpu as pltpu
from jax.sharding import PartitionSpec as P

KX = 16
KY = 16
K = KX * KY
ORB = 16
W = 8
PASSES = 3
NZ, NY = 8, 4
CHIPS = NZ * NY
CORES = 2
TM = 4
HERE = 4
LANES = W * ORB
QUARTER = LANES // 4
HALF = LANES // 2
BLOCKS = 4

MESH = pl.DeviceIdType.MESH
F32 = jnp.float32
BF16 = jnp.bfloat16


PAIRS = K // 2 - 2


def momentum_tables():
    place = np.arange(K)
    parted = 4 * (place // 2 % (K // 4)) + place % 2 + 2 * (place // (K // 2))
    minus = (-(place // KY)) % KX * KY + (-(place % KY)) % KY
    alone = place[minus == place]
    upper = place[place < minus]

    def waves(rows, columns):
        turn = (rows[:, None] // KY) * (columns[None, :] // KY) % KX
        turn = turn + (rows[:, None] % KY) * (columns[None, :] % KY) % KY
        phase = 2.0 * math.pi * turn / 16.0
        return np.cos(phase) / 16.0, np.sin(phase) / 16.0

    def table(momenta):
        cosine, sine = waves(upper, momenta)
        lone = waves(alone, momenta)[0]
        return np.concatenate([cosine, lone[:2], sine, lone[2:]], axis=0).astype(np.float32)

    def parts(full):
        high = full.astype(ml_dtypes.bfloat16)
        low = (full - high.astype(np.float32)).astype(ml_dtypes.bfloat16)
        return np.stack([high, low])

    return parts(table(parted).T), parts(table(place))


def split(x):
    high = x.astype(BF16)
    return high, (x - high.astype(F32)).astype(BF16)


def mm(a, b):
    return jnp.dot(a, b, preferred_element_type=F32)


def ring(step, size):
    return min(step % size, -step % size)


PLACES = [
    (dz, dy, flip)
    for dz, dy in sorted(
        ((dz, dy) for dz in range(NZ) for dy in range(NY)), key=lambda o: -(ring(o[0], NZ) + ring(o[1], NY))
    )
    for flip in (1, 0)
]


def kernel(
    hl, hr, prop_hbm, coup_hbm, mf_hbm, lag_hbm, ahead_hbm, back_hbm,
    out,
    prop, coup, mf, lag, hlv, hrv, ahead, backward, startv, hank, sendf, fbuf, sendb, rbuf,
    load_sem, x_send, x_recv, f_send, f_recv, f_own, b_send, b_recv,
):
    dev = lax.axis_index("mom")
    x = lax.axis_index("tm")
    core = lax.rem(dev, CORES)
    chip = dev // CORES
    z = chip // NY
    y = lax.rem(chip, NY)
    last = TM - 1
    others = CHIPS * CORES - 1
    row = chip // 2
    quarter = lax.rem(chip, 2) * 2 + core
    far_z = [lax.rem(z + dz, NZ) * (NY * CORES) for dz in range(NZ)]
    far_y = [lax.rem(y + dy, NY) * CORES for dy in range(NY)]
    far_core = [core, 1 - core]

    def at_place(place):
        dz, dy, flip = place
        return far_z[dz] + far_y[dy] + far_core[flip]

    def device(goal, plane):
        return {"mom": goal, "tm": plane}

    small = [
        pltpu.make_async_copy(source, target, load_sem.at[4 + number])
        for number, (source, target) in enumerate(
            ((prop_hbm, prop), (coup_hbm, coup), (mf_hbm, mf), (lag_hbm, lag))
        )
    ]
    loads = [
        pltpu.make_async_copy(hl, hlv.at[:, :, :, pl.ds(LANES, BLOCKS * LANES)], load_sem.at[0]),
        pltpu.make_async_copy(hr, hrv.at[:, :, :, pl.ds(LANES, BLOCKS * LANES)], load_sem.at[1]),
    ]
    tables_in = [
        pltpu.make_async_copy(ahead_hbm, ahead, load_sem.at[2]),
        pltpu.make_async_copy(back_hbm, backward, load_sem.at[3]),
    ]

    for load in small + loads + tables_in:
        load.start()
    barrier = pltpu.get_barrier_semaphore()

    def greet(goal, plane):
        pl.semaphore_signal(barrier, inc=1, device_id=device(goal, plane), device_id_type=MESH)

    @pl.when(x < last)
    def _():
        for place in PLACES:
            greet(at_place(place), last)

    for place in PLACES[:-1]:
        greet(at_place(place), x)

    @pl.when(x > 0)
    def _():
        greet(dev, x - 1)

    for load in small:
        load.wait()

    lane = lax.broadcasted_iota(jnp.int32, (1, LANES), 1)
    block_of_lane = lane // QUARTER

    column = lax.broadcasted_iota(jnp.int32, (QUARTER, K), 0)
    point = lax.broadcasted_iota(jnp.int32, (QUARTER, K), 1)
    strength = jnp.zeros((QUARTER, K), F32)
    mf_term = jnp.zeros((QUARTER, K), F32)
    for b in range(ORB):
        here = lax.rem(column, ORB) == b
        strength = jnp.where(here, coup[row * ORB + b], strength)
        mf_term = jnp.where(here, mf[row * ORB + b], mf_term)
    strength = strength * strength
    mf_term = jnp.where((point == PAIRS) & (column >= ORB) & (quarter == 3), mf_term, 0.0)
    lone = lane >= PAIRS

    def transpose_blocks(parts):
        result = []
        for j in range(4):
            total = parts[j]
            for i in range(4):
                if i == j:
                    continue
                moved = pltpu.roll(parts[i], (QUARTER * (i - j)) % LANES, 1)
                total = jnp.where(block_of_lane == i, moved, total)
            result.append(total)
        return result

    def start_block(block):
        at = pl.ds(block * LANES, LANES)
        for k in range(HERE):
            stack = jnp.concatenate([prop[0, k], prop[1, k]], axis=0)
            real, imag = (
                jnp.dot(
                    stack, hlv[c, k, :, pl.ds((block + 1) * LANES, LANES)],
                    precision=lax.Precision.HIGHEST, preferred_element_type=F32,
                )
                for c in range(2)
            )
            startv[0, k, :, at] = real[:ORB] - imag[ORB:]
            startv[1, k, :, at] = real[ORB:] + imag[:ORB]

    def build(k, slot, source_r, source_l, lanes_from):
        for lp, source in enumerate((source_r, source_l)):
            for c in range(2):
                first = source[c, k, :, pl.ds(lanes_from, LANES)]
                second = source[c, k, :, pl.ds(lanes_from + LANES, LANES)]
                for m in range(W):
                    shift = ORB * (m + 1)
                    if shift < LANES:
                        moved = pltpu.roll(jnp.where(lane >= shift, first, second), LANES - shift, 1)
                    else:
                        moved = second
                    high, low = split(moved * lag[m])
                    at = lp * LANES + m * ORB
                    hank[slot, 0, pl.ds(at, ORB), pl.ds(c * LANES, LANES)] = high
                    hank[slot, 1, pl.ds(at, ORB), pl.ds(c * LANES, LANES)] = low

    def build_blocks(blocks):
        @pl.loop(0, HERE)
        def _(k):
            for block in blocks:
                build(k, block * HERE + k, hrv, hlv, block * LANES)

    def pack_window(p, reals, imags):
        for r in range(2):
            parts = transpose_blocks([reals[r], imags[r], reals[r + 2], imags[r + 2]])
            for w in range(4):
                sendf[p, pl.ds(2 * w + r, ORB, stride=8), :] = parts[w]

    def forward_copy(p, place, plane):
        goal = at_place(place)
        return pltpu.make_async_remote_copy(
            src_ref=sendf.at[p, pl.ds(goal * 2, 2), :], dst_ref=fbuf.at[p, pl.ds(dev * 2, 2), :],
            send_sem=f_send.at[p], recv_sem=f_recv.at[p],
            device_id=device(goal, plane), device_id_type=MESH,
        )

    def own_forward(p):
        here = pl.ds(dev * 2, 2)
        return pltpu.make_async_copy(sendf.at[p, here, :], fbuf.at[p, here, :], f_own.at[p])

    def back_copy(p, place):
        goal = at_place(place)
        return pltpu.make_async_remote_copy(
            src_ref=sendb.at[p, pl.ds(goal * HERE, HERE), :], dst_ref=rbuf.at[p, pl.ds(dev * HERE, HERE), :],
            send_sem=b_send.at[p], recv_sem=b_recv.at[p],
            device_id=device(goal, x), device_id_type=MESH,
        )

    def own_back(p):
        here = pl.ds(dev * HERE, HERE)
        return pltpu.make_async_copy(sendb.at[p, here, :], rbuf.at[p, here, :], f_own.at[PASSES + p])

    def wait_rows(rows, sem):
        while rows:
            some = sendb.at[0, pl.ds(0, min(rows, K)), :]
            pltpu.make_async_copy(some, some, sem).wait()
            rows -= min(rows, K)

    def send_forward(p):
        if p == PASSES - 1:
            for plane in range(last):
                for place in PLACES:
                    forward_copy(p, place, plane).start()
        own_forward(p).start()
        for place in PLACES[:-1]:
            forward_copy(p, place, last).start()

    def wait_forward(p):
        own_forward(p).wait()
        wait_rows(others * 2, f_recv.at[p])

    def real_space(p):
        turned = fbuf[p].T
        value = jnp.concatenate([turned[:HALF], turned[HALF:]], axis=1)
        high, low = split(value)
        product = mm(jnp.concatenate([high, low], axis=0), ahead[0])
        product = product[:HALF] + product[HALF:] + mm(high, ahead[1])
        even, odd = product[:, :LANES], product[:, LANES:]
        crossed = jnp.concatenate([-odd[QUARTER:], odd[:QUARTER]], axis=0)
        pos = jnp.concatenate(
            [jnp.where(lone, even, even + crossed), jnp.where(lone, odd, even - crossed)], axis=1
        )
        real, imag = pos[:QUARTER], pos[QUARTER:]
        square_real, square_imag = real * real, imag * imag
        factor = strength * (square_real + square_imag) + mf_term
        twice = 2.0 * strength
        both = jnp.concatenate(
            [factor * real, factor * imag, strength * (square_real - square_imag), twice * real * imag],
            axis=0,
        )
        first, second = both[:, :LANES], both[:, LANES:]
        change = first - second
        crossed = jnp.concatenate(
            [
                change[QUARTER : 2 * QUARTER],
                -change[:QUARTER],
                change[3 * QUARTER :],
                -change[2 * QUARTER : 3 * QUARTER],
            ],
            axis=0,
        )
        value = jnp.concatenate(
            [jnp.where(lone, first, first + second), jnp.where(lone, second, crossed)], axis=1
        )
        high, low = split(value)
        product = mm(jnp.concatenate([high, low], axis=0), backward[0])
        product = product[:LANES] + product[LANES:] + mm(high, backward[1])
        sendb[p, pl.ds(0, LANES), :] = product[:, :LANES].T
        sendb[p, pl.ds(LANES, LANES), :] = product[:, LANES:].T

    def send_back(p):
        own_back(p).start()
        for place in PLACES[:-1]:
            back_copy(p, place).start()

    def wait_back(p):
        own_back(p).wait()
        wait_rows(others * HERE, b_recv.at[p])

    def arrived(p, k):
        parts = transpose_blocks([rbuf[p, pl.ds(w * HERE + k, ORB, stride=4 * HERE), :] for w in range(4)])
        lesser_real, lesser_imag, pair_real, pair_imag = parts
        high, low = split(
            jnp.concatenate(
                [
                    jnp.concatenate([lesser_real, pair_real], axis=1),
                    jnp.concatenate([lesser_imag, pair_imag], axis=1),
                ],
                axis=0,
            )
        )
        return jnp.concatenate([high, low], axis=0)

    def collide(stack, slot):
        rows = 2 * ORB
        product = mm(stack, hank[slot, 0])
        total = product[:rows] + product[rows:] + mm(stack[:rows], hank[slot, 1])
        real = total[:ORB, :LANES] - total[ORB:, LANES:]
        imag = total[:ORB, LANES:] + total[ORB:, :LANES]
        return real, imag

    def rim_copy(part):
        src, dst = ((hl, hlv), (hr, hrv))[part]
        return pltpu.make_async_remote_copy(
            src_ref=src.at[:, :, :, pl.ds((BLOCKS - 1) * LANES, LANES)],
            dst_ref=dst.at[:, :, :, pl.ds(0, LANES)],
            send_sem=x_send.at[part], recv_sem=x_recv.at[part],
            device_id=device(dev, lax.rem(x + 1, TM)), device_id_type=MESH,
        )

    for load in loads:
        load.wait()
    start_block(BLOCKS - 1)
    newest_times = pl.ds((BLOCKS - 1) * LANES, LANES)

    @pl.when(x == last)
    def _():
        pack_window(0, *([startv[c, k, :, newest_times] for k in range(HERE)] for c in range(2)))
        pl.semaphore_wait(barrier, others + last * (others + 1))
        send_forward(0)

    @pl.when(x < last)
    def _():
        pl.semaphore_wait(barrier, others + 1)
        for part in range(2):
            rim_copy(part).start()

    @pl.when(x == 0)
    def _():
        zeros = jnp.zeros((2, HERE, ORB, LANES), F32)
        hlv[:, :, :, pl.ds(0, LANES)] = zeros
        hrv[:, :, :, pl.ds(0, LANES)] = zeros

    build_blocks((BLOCKS - 1,))
    for block in range(BLOCKS - 1):
        start_block(block)
    for load in tables_in:
        load.wait()

    @pl.when(x == last)
    def _():
        for p in range(PASSES - 1):
            if p:
                build_blocks((2,))
            wait_forward(p)
            real_space(p)
            send_back(p)
            if p == 0:
                build_blocks((1,))
            wait_back(p)
            reals, imags = [], []
            for k in range(HERE):
                real, imag = collide(arrived(p, k), (BLOCKS - 1) * HERE + k)
                reals.append(startv[0, k, :, newest_times] + imag)
                imags.append(startv[1, k, :, newest_times] - real)
            pack_window(p + 1, reals, imags)
            send_forward(p + 1)

    @pl.when(x < last)
    def _():
        build_blocks((1, 2))

    @pl.when(x > 0)
    def _():
        for part in range(2):
            rim_copy(part).wait_recv()

    build_blocks((0,))

    p = PASSES - 1

    @pl.when(x == last)
    def _():
        wait_forward(p)

    @pl.when(x < last)
    def _():
        wait_rows((others + 1) * 2, f_recv.at[p])

    real_space(p)
    send_back(p)
    wait_back(p)
    for k in range(HERE):
        stack = arrived(p, k)
        for block in range(BLOCKS):
            real, imag = collide(stack, block * HERE + k)
            at = pl.ds(block * LANES, LANES)
            out[0, k, :, at] = startv[0, k, :, at] + imag
            out[1, k, :, at] = startv[1, k, :, at] - real

    wait_rows(others * HERE, b_send.at[p])

    @pl.when(x == last)
    def _():
        for p in range(PASSES - 1):
            wait_rows(others * HERE, b_send.at[p])
            wait_rows(others * 2, f_send.at[p])
        wait_rows((others + last * (others + 1)) * 2, f_send.at[PASSES - 1])

    @pl.when(x < last)
    def _():
        for part in range(2):
            rim_copy(part).wait_send()


def on_device(ahead, back, hist_lesser, hist_retarded, propagator, coupling, mf_weight, lag_weight):
    vmem = pl.BlockSpec(memory_space=pltpu.VMEM)
    hbm = pl.BlockSpec(memory_space=pltpu.HBM)
    padded = (2, HERE, ORB, (BLOCKS + 1) * LANES)
    return pl.pallas_call(
        kernel,
        out_shape=pltpu.VMEM(hist_lesser.shape, F32),
        in_specs=[hbm] * 8,
        out_specs=vmem,
        scratch_shapes=[
            pltpu.VMEM((2, HERE, ORB, ORB), F32),
            pltpu.SMEM((ORB * ORB,), F32),
            pltpu.SMEM((ORB * ORB,), F32),
            pltpu.SMEM((W,), F32),
            pltpu.VMEM(padded, F32),
            pltpu.VMEM(padded, F32),
            pltpu.VMEM((2, K, K), BF16),
            pltpu.VMEM((2, K, K), BF16),
            pltpu.VMEM((2, HERE, ORB, BLOCKS * LANES), F32),
            pltpu.VMEM((BLOCKS * HERE, 2, 2 * LANES, 2 * LANES), BF16),
            pltpu.VMEM((PASSES, K // 2, LANES), F32),
            pltpu.VMEM((PASSES, K // 2, LANES), F32),
            pltpu.VMEM((PASSES, K, LANES), F32),
            pltpu.VMEM((PASSES, K, LANES), F32),
            pltpu.SemaphoreType.DMA((8,)),
            pltpu.SemaphoreType.DMA((2,)),
            pltpu.SemaphoreType.DMA((2,)),
            pltpu.SemaphoreType.DMA((PASSES,)),
            pltpu.SemaphoreType.DMA((PASSES,)),
            pltpu.SemaphoreType.DMA((2 * PASSES,)),
            pltpu.SemaphoreType.DMA((PASSES,)),
            pltpu.SemaphoreType.DMA((PASSES,)),
        ],
        compiler_params=pltpu.CompilerParams(
            collective_id=0, has_side_effects=True, vmem_limit_bytes=67043328 - 4 * math.prod(hist_lesser.shape)
        ),
    )(hist_lesser, hist_retarded, propagator, coupling, mf_weight, lag_weight, ahead, back)


def solution(mesh):
    tables = momentum_tables()

    def step(*args):
        return jax.shard_map(
            on_device,
            mesh=mesh,
            in_specs=(
                P(None, None, None),
                P(None, None, None),
                P(None, "mom", None, "tm"),
                P(None, "mom", None, "tm"),
                P(None, "mom", None, None),
                P(),
                P(),
                P(),
            ),
            out_specs=P(None, "mom", None, "tm"),
            check_vma=False,
        )(*map(jnp.asarray, tables), *args)

    return step
```

```python
import math

import jax
import jax.numpy as jnp
import ml_dtypes
import numpy as np
from jax import lax
from jax.experimental import pallas as pl
from jax.experimental.pallas import tpu as pltpu
from jax.sharding import PartitionSpec as P

KX = 16
KY = 16
K = KX * KY
ORB = 16
W = 8
PASSES = 3
NZ, NY = 8, 4
CHIPS = NZ * NY
CORES = 2
TM = 4
HERE = 4
LANES = W * ORB
QUARTER = LANES // 4
HALF = LANES // 2
BLOCKS = 4

MESH = pl.DeviceIdType.MESH
F32 = jnp.float32
BF16 = jnp.bfloat16


PAIRS = K // 2 - 2


def momentum_tables():
    place = np.arange(K)
    parted = 4 * (place // 2 % (K // 4)) + place % 2 + 2 * (place // (K // 2))
    minus = (-(place // KY)) % KX * KY + (-(place % KY)) % KY
    alone = place[minus == place]
    upper = place[place < minus]

    def waves(rows, columns):
        turn = (rows[:, None] // KY) * (columns[None, :] // KY) % KX
        turn = turn + (rows[:, None] % KY) * (columns[None, :] % KY) % KY
        phase = 2.0 * math.pi * turn / 16.0
        return np.cos(phase) / 16.0, np.sin(phase) / 16.0

    def table(momenta):
        cosine, sine = waves(upper, momenta)
        lone = waves(alone, momenta)[0]
        return np.concatenate([cosine, lone[:2], sine, lone[2:]], axis=0).astype(np.float32)

    def parts(full):
        high = full.astype(ml_dtypes.bfloat16)
        low = (full - high.astype(np.float32)).astype(ml_dtypes.bfloat16)
        return np.stack([high, low])

    return parts(table(parted).T), parts(table(place))


def split(x):
    high = x.astype(BF16)
    return high, (x - high.astype(F32)).astype(BF16)


def mm(a, b):
    return jnp.dot(a, b, preferred_element_type=F32)


def ring(step, size):
    return min(step % size, -step % size)


PLACES = [
    (dz, dy, flip)
    for dz, dy in sorted(
        ((dz, dy) for dz in range(NZ) for dy in range(NY)), key=lambda o: -(ring(o[0], NZ) + ring(o[1], NY))
    )
    for flip in (1, 0)
]


def kernel(
    hl, hr, prop_hbm, coup_hbm, mf_hbm, lag_hbm, ahead_hbm, back_hbm,
    out,
    prop, coup, mf, lag, hlv, hrv, ahead, backward, startv, hank, sendf, fbuf, sendb, rbuf,
    load_sem, x_send, x_recv, f_send, f_recv, f_own, b_send, b_recv, ready,
):
    dev = lax.axis_index("mom")
    x = lax.axis_index("tm")
    core = lax.rem(dev, CORES)
    chip = dev // CORES
    z = chip // NY
    y = lax.rem(chip, NY)
    last = TM - 1
    others = CHIPS * CORES - 1
    row = chip // 2
    quarter = lax.rem(chip, 2) * 2 + core
    far_z = [lax.rem(z + dz, NZ) * (NY * CORES) for dz in range(NZ)]
    far_y = [lax.rem(y + dy, NY) * CORES for dy in range(NY)]
    far_core = [core, 1 - core]

    def at_place(place):
        dz, dy, flip = place
        return far_z[dz] + far_y[dy] + far_core[flip]

    def device(goal, plane):
        return {"mom": goal, "tm": plane}

    small = [
        pltpu.make_async_copy(source, target, load_sem.at[4 + number])
        for number, (source, target) in enumerate(
            ((prop_hbm, prop), (coup_hbm, coup), (mf_hbm, mf), (lag_hbm, lag))
        )
    ]
    loads = [
        pltpu.make_async_copy(hl, hlv.at[:, :, :, pl.ds(LANES, BLOCKS * LANES)], load_sem.at[0]),
        pltpu.make_async_copy(hr, hrv.at[:, :, :, pl.ds(LANES, BLOCKS * LANES)], load_sem.at[1]),
    ]
    tables_in = [
        pltpu.make_async_copy(ahead_hbm, ahead, load_sem.at[2]),
        pltpu.make_async_copy(back_hbm, backward, load_sem.at[3]),
    ]

    for load in small + loads + tables_in:
        load.start()
    barrier = pltpu.get_barrier_semaphore()

    def greet(goal, plane):
        pl.semaphore_signal(barrier, inc=1, device_id=device(goal, plane), device_id_type=MESH)

    for place in PLACES[:-1]:
        greet(at_place(place), x)

    @pl.when(x > 0)
    def _():
        greet(dev, x - 1)

    @pl.when(x == last)
    def _():
        for plane in range(last - 1):
            greet(dev, plane)

    for load in small:
        load.wait()

    lane = lax.broadcasted_iota(jnp.int32, (1, LANES), 1)
    block_of_lane = lane // QUARTER

    column = lax.broadcasted_iota(jnp.int32, (QUARTER, K), 0)
    point = lax.broadcasted_iota(jnp.int32, (QUARTER, K), 1)
    strength = jnp.zeros((QUARTER, K), F32)
    mf_term = jnp.zeros((QUARTER, K), F32)
    for b in range(ORB):
        here = lax.rem(column, ORB) == b
        strength = jnp.where(here, coup[row * ORB + b], strength)
        mf_term = jnp.where(here, mf[row * ORB + b], mf_term)
    strength = strength * strength
    mf_term = jnp.where((point == PAIRS) & (column >= ORB) & (quarter == 3), mf_term, 0.0)
    lone = lane >= PAIRS

    def transpose_blocks(parts):
        result = []
        for j in range(4):
            total = parts[j]
            for i in range(4):
                if i == j:
                    continue
                moved = pltpu.roll(parts[i], (QUARTER * (i - j)) % LANES, 1)
                total = jnp.where(block_of_lane == i, moved, total)
            result.append(total)
        return result

    def start_block(block):
        at = pl.ds(block * LANES, LANES)
        for k in range(HERE):
            stack = jnp.concatenate([prop[0, k], prop[1, k]], axis=0)
            real, imag = (
                jnp.dot(
                    stack, hlv[c, k, :, pl.ds((block + 1) * LANES, LANES)],
                    precision=lax.Precision.HIGHEST, preferred_element_type=F32,
                )
                for c in range(2)
            )
            startv[0, k, :, at] = real[:ORB] - imag[ORB:]
            startv[1, k, :, at] = real[ORB:] + imag[:ORB]

    def build(k, slot, source_r, source_l, lanes_from):
        for lp, source in enumerate((source_r, source_l)):
            for c in range(2):
                first = source[c, k, :, pl.ds(lanes_from, LANES)]
                second = source[c, k, :, pl.ds(lanes_from + LANES, LANES)]
                for m in range(W):
                    shift = ORB * (m + 1)
                    if shift < LANES:
                        moved = pltpu.roll(jnp.where(lane >= shift, first, second), LANES - shift, 1)
                    else:
                        moved = second
                    high, low = split(moved * lag[m])
                    at = lp * LANES + m * ORB
                    hank[slot, 0, pl.ds(at, ORB), pl.ds(c * LANES, LANES)] = high
                    hank[slot, 1, pl.ds(at, ORB), pl.ds(c * LANES, LANES)] = low

    def build_blocks(blocks):
        @pl.loop(0, HERE)
        def _(k):
            for block in blocks:
                build(k, block * HERE + k, hrv, hlv, block * LANES)

    def pack_window(p, reals, imags):
        for r in range(2):
            parts = transpose_blocks([reals[r], imags[r], reals[r + 2], imags[r + 2]])
            for w in range(4):
                sendf[p, pl.ds(2 * w + r, ORB, stride=8), :] = parts[w]

    def forward_copy(p, place, plane):
        goal = at_place(place)
        return pltpu.make_async_remote_copy(
            src_ref=sendf.at[p, pl.ds(goal * 2, 2), :], dst_ref=fbuf.at[p, pl.ds(dev * 2, 2), :],
            send_sem=f_send.at[p], recv_sem=f_recv.at[p],
            device_id=device(goal, plane), device_id_type=MESH,
        )

    def own_forward(p):
        here = pl.ds(dev * 2, 2)
        return pltpu.make_async_copy(sendf.at[p, here, :], fbuf.at[p, here, :], f_own.at[p])

    def back_copy(p, place):
        goal = at_place(place)
        return pltpu.make_async_remote_copy(
            src_ref=sendb.at[p, pl.ds(goal * HERE, HERE), :], dst_ref=rbuf.at[p, pl.ds(dev * HERE, HERE), :],
            send_sem=b_send.at[p], recv_sem=b_recv.at[p],
            device_id=device(goal, x), device_id_type=MESH,
        )

    def own_back(p):
        here = pl.ds(dev * HERE, HERE)
        return pltpu.make_async_copy(sendb.at[p, here, :], rbuf.at[p, here, :], f_own.at[PASSES + p])

    def wait_rows(rows, sem):
        while rows:
            some = sendb.at[0, pl.ds(0, min(rows, K)), :]
            pltpu.make_async_copy(some, some, sem).wait()
            rows -= min(rows, K)

    def send_forward(p):
        if p == PASSES - 1:
            pl.semaphore_wait(ready, last)
            for plane in range(last):
                for place in PLACES:
                    forward_copy(p, place, plane).start()
        own_forward(p).start()
        for place in PLACES[:-1]:
            forward_copy(p, place, last).start()

    def wait_forward(p):
        own_forward(p).wait()
        wait_rows(others * 2, f_recv.at[p])

    def real_space(p):
        turned = fbuf[p].T
        value = jnp.concatenate([turned[:HALF], turned[HALF:]], axis=1)
        high, low = split(value)
        product = mm(jnp.concatenate([high, low], axis=0), ahead[0])
        product = product[:HALF] + product[HALF:] + mm(high, ahead[1])
        even, odd = product[:, :LANES], product[:, LANES:]
        crossed = jnp.concatenate([-odd[QUARTER:], odd[:QUARTER]], axis=0)
        pos = jnp.concatenate(
            [jnp.where(lone, even, even + crossed), jnp.where(lone, odd, even - crossed)], axis=1
        )
        real, imag = pos[:QUARTER], pos[QUARTER:]
        square_real, square_imag = real * real, imag * imag
        factor = strength * (square_real + square_imag) + mf_term
        twice = 2.0 * strength
        both = jnp.concatenate(
            [factor * real, factor * imag, strength * (square_real - square_imag), twice * real * imag],
            axis=0,
        )
        first, second = both[:, :LANES], both[:, LANES:]
        change = first - second
        crossed = jnp.concatenate(
            [
                change[QUARTER : 2 * QUARTER],
                -change[:QUARTER],
                change[3 * QUARTER :],
                -change[2 * QUARTER : 3 * QUARTER],
            ],
            axis=0,
        )
        value = jnp.concatenate(
            [jnp.where(lone, first, first + second), jnp.where(lone, second, crossed)], axis=1
        )
        high, low = split(value)
        product = mm(jnp.concatenate([high, low], axis=0), backward[0])
        product = product[:LANES] + product[LANES:] + mm(high, backward[1])
        sendb[p, pl.ds(0, LANES), :] = product[:, :LANES].T
        sendb[p, pl.ds(LANES, LANES), :] = product[:, LANES:].T

    def send_back(p):
        own_back(p).start()
        for place in PLACES[:-1]:
            back_copy(p, place).start()

    def wait_back(p):
        own_back(p).wait()
        wait_rows(others * HERE, b_recv.at[p])

    def arrived(p, k):
        parts = transpose_blocks([rbuf[p, pl.ds(w * HERE + k, ORB, stride=4 * HERE), :] for w in range(4)])
        lesser_real, lesser_imag, pair_real, pair_imag = parts
        high, low = split(
            jnp.concatenate(
                [
                    jnp.concatenate([lesser_real, pair_real], axis=1),
                    jnp.concatenate([lesser_imag, pair_imag], axis=1),
                ],
                axis=0,
            )
        )
        return jnp.concatenate([high, low], axis=0)

    def collide(stack, slot):
        rows = 2 * ORB
        product = mm(stack, hank[slot, 0])
        total = product[:rows] + product[rows:] + mm(stack[:rows], hank[slot, 1])
        real = total[:ORB, :LANES] - total[ORB:, LANES:]
        imag = total[:ORB, LANES:] + total[ORB:, :LANES]
        return real, imag

    def rim_copy(part):
        src, dst = ((hl, hlv), (hr, hrv))[part]
        return pltpu.make_async_remote_copy(
            src_ref=src.at[:, :, :, pl.ds((BLOCKS - 1) * LANES, LANES)],
            dst_ref=dst.at[:, :, :, pl.ds(0, LANES)],
            send_sem=x_send.at[part], recv_sem=x_recv.at[part],
            device_id=device(dev, lax.rem(x + 1, TM)), device_id_type=MESH,
        )

    for load in loads:
        load.wait()
    start_block(BLOCKS - 1)
    newest_times = pl.ds((BLOCKS - 1) * LANES, LANES)

    @pl.when(x == last)
    def _():
        pack_window(0, *([startv[c, k, :, newest_times] for k in range(HERE)] for c in range(2)))
        pl.semaphore_wait(barrier, others)
        send_forward(0)

    @pl.when(x == last - 1)
    def _():
        pl.semaphore_wait(barrier, others + 1)

    @pl.when(x < last - 1)
    def _():
        pl.semaphore_wait(barrier, others + 2)

    @pl.when(x < last)
    def _():
        pl.semaphore_signal(ready, inc=1, device_id=device(dev, last), device_id_type=MESH)
        for part in range(2):
            rim_copy(part).start()

    @pl.when(x == 0)
    def _():
        zeros = jnp.zeros((2, HERE, ORB, LANES), F32)
        hlv[:, :, :, pl.ds(0, LANES)] = zeros
        hrv[:, :, :, pl.ds(0, LANES)] = zeros

    build_blocks((BLOCKS - 1,))
    for block in range(BLOCKS - 1):
        start_block(block)
    for load in tables_in:
        load.wait()

    @pl.when(x == last)
    def _():
        for p in range(PASSES - 1):
            if p:
                build_blocks((2,))
            wait_forward(p)
            real_space(p)
            send_back(p)
            if p == 0:
                build_blocks((1,))
            wait_back(p)
            reals, imags = [], []
            for k in range(HERE):
                real, imag = collide(arrived(p, k), (BLOCKS - 1) * HERE + k)
                reals.append(startv[0, k, :, newest_times] + imag)
                imags.append(startv[1, k, :, newest_times] - real)
            pack_window(p + 1, reals, imags)
            send_forward(p + 1)

    @pl.when(x < last)
    def _():
        build_blocks((1, 2))

    @pl.when(x > 0)
    def _():
        for part in range(2):
            rim_copy(part).wait_recv()

    build_blocks((0,))

    p = PASSES - 1

    @pl.when(x == last)
    def _():
        wait_forward(p)

    @pl.when(x < last)
    def _():
        wait_rows((others + 1) * 2, f_recv.at[p])

    real_space(p)
    send_back(p)
    wait_back(p)
    for k in range(HERE):
        stack = arrived(p, k)
        for block in range(BLOCKS):
            real, imag = collide(stack, block * HERE + k)
            at = pl.ds(block * LANES, LANES)
            out[0, k, :, at] = startv[0, k, :, at] + imag
            out[1, k, :, at] = startv[1, k, :, at] - real

    wait_rows(others * HERE, b_send.at[p])

    @pl.when(x == last)
    def _():
        for p in range(PASSES - 1):
            wait_rows(others * HERE, b_send.at[p])
            wait_rows(others * 2, f_send.at[p])
        wait_rows((others + last * (others + 1)) * 2, f_send.at[PASSES - 1])

    @pl.when(x < last)
    def _():
        for part in range(2):
            rim_copy(part).wait_send()


def on_device(ahead, back, hist_lesser, hist_retarded, propagator, coupling, mf_weight, lag_weight):
    vmem = pl.BlockSpec(memory_space=pltpu.VMEM)
    hbm = pl.BlockSpec(memory_space=pltpu.HBM)
    padded = (2, HERE, ORB, (BLOCKS + 1) * LANES)
    return pl.pallas_call(
        kernel,
        out_shape=pltpu.VMEM(hist_lesser.shape, F32),
        in_specs=[hbm] * 8,
        out_specs=vmem,
        scratch_shapes=[
            pltpu.VMEM((2, HERE, ORB, ORB), F32),
            pltpu.SMEM((ORB * ORB,), F32),
            pltpu.SMEM((ORB * ORB,), F32),
            pltpu.SMEM((W,), F32),
            pltpu.VMEM(padded, F32),
            pltpu.VMEM(padded, F32),
            pltpu.VMEM((2, K, K), BF16),
            pltpu.VMEM((2, K, K), BF16),
            pltpu.VMEM((2, HERE, ORB, BLOCKS * LANES), F32),
            pltpu.VMEM((BLOCKS * HERE, 2, 2 * LANES, 2 * LANES), BF16),
            pltpu.VMEM((PASSES, K // 2, LANES), F32),
            pltpu.VMEM((PASSES, K // 2, LANES), F32),
            pltpu.VMEM((PASSES, K, LANES), F32),
            pltpu.VMEM((PASSES, K, LANES), F32),
            pltpu.SemaphoreType.DMA((8,)),
            pltpu.SemaphoreType.DMA((2,)),
            pltpu.SemaphoreType.DMA((2,)),
            pltpu.SemaphoreType.DMA((PASSES,)),
            pltpu.SemaphoreType.DMA((PASSES,)),
            pltpu.SemaphoreType.DMA((2 * PASSES,)),
            pltpu.SemaphoreType.DMA((PASSES,)),
            pltpu.SemaphoreType.DMA((PASSES,)),
            pltpu.SemaphoreType.REGULAR,
        ],
        compiler_params=pltpu.CompilerParams(
            collective_id=0, has_side_effects=True, vmem_limit_bytes=67043328 - 4 * math.prod(hist_lesser.shape)
        ),
    )(hist_lesser, hist_retarded, propagator, coupling, mf_weight, lag_weight, ahead, back)


def solution(mesh):
    tables = momentum_tables()

    def step(*args):
        return jax.shard_map(
            on_device,
            mesh=mesh,
            in_specs=(
                P(None, None, None),
                P(None, None, None),
                P(None, "mom", None, "tm"),
                P(None, "mom", None, "tm"),
                P(None, "mom", None, None),
                P(),
                P(),
                P(),
            ),
            out_specs=P(None, "mom", None, "tm"),
            check_vma=False,
        )(*map(jnp.asarray, tables), *args)

    return step
```

```python
import math

import jax
import jax.numpy as jnp
import ml_dtypes
import numpy as np
from jax import lax
from jax.experimental import pallas as pl
from jax.experimental.pallas import tpu as pltpu
from jax.sharding import PartitionSpec as P

KX = 16
KY = 16
K = KX * KY
ORB = 16
W = 8
PASSES = 3
NZ, NY = 8, 4
CHIPS = NZ * NY
CORES = 2
TM = 4
HERE = 4
LANES = W * ORB
QUARTER = LANES // 4
HALF = LANES // 2
BLOCKS = 4

MESH = pl.DeviceIdType.MESH
F32 = jnp.float32
BF16 = jnp.bfloat16


PAIRS = K // 2 - 2


def momentum_tables():
    place = np.arange(K)
    parted = 4 * (place // 2 % (K // 4)) + place % 2 + 2 * (place // (K // 2))
    minus = (-(place // KY)) % KX * KY + (-(place % KY)) % KY
    alone = place[minus == place]
    upper = place[place < minus]

    def waves(rows, columns):
        turn = (rows[:, None] // KY) * (columns[None, :] // KY) % KX
        turn = turn + (rows[:, None] % KY) * (columns[None, :] % KY) % KY
        phase = 2.0 * math.pi * turn / 16.0
        return np.cos(phase) / 16.0, np.sin(phase) / 16.0

    def table(momenta):
        cosine, sine = waves(upper, momenta)
        lone = waves(alone, momenta)[0]
        return np.concatenate([cosine, lone[:2], sine, lone[2:]], axis=0).astype(np.float32)

    def parts(full):
        high = full.astype(ml_dtypes.bfloat16)
        low = (full - high.astype(np.float32)).astype(ml_dtypes.bfloat16)
        return np.stack([high, low])

    return parts(table(parted).T), parts(table(place))


def split(x):
    high = x.astype(BF16)
    return high, (x - high.astype(F32)).astype(BF16)


def mm(a, b):
    return jnp.dot(a, b, preferred_element_type=F32)


def ring(step, size):
    return min(step % size, -step % size)


PLACES = [
    (dz, dy, flip)
    for dz, dy in sorted(
        ((dz, dy) for dz in range(NZ) for dy in range(NY)), key=lambda o: -(ring(o[0], NZ) + ring(o[1], NY))
    )
    for flip in (1, 0)
]


def kernel(
    hl, hr, prop_hbm, coup_hbm, mf_hbm, lag_hbm, ahead_hbm, back_hbm,
    out,
    prop, coup, mf, lag, hlv, hrv, ahead, backward, startv, hank, sendf, fbuf, sendb, rbuf,
    load_sem, x_send, x_recv, f_send, f_recv, f_own, b_send, b_recv, ready,
):
    dev = lax.axis_index("mom")
    x = lax.axis_index("tm")
    core = lax.rem(dev, CORES)
    chip = dev // CORES
    z = chip // NY
    y = lax.rem(chip, NY)
    last = TM - 1
    others = CHIPS * CORES - 1
    row = chip // 2
    quarter = lax.rem(chip, 2) * 2 + core
    far_z = [lax.rem(z + dz, NZ) * (NY * CORES) for dz in range(NZ)]
    far_y = [lax.rem(y + dy, NY) * CORES for dy in range(NY)]
    far_core = [core, 1 - core]

    def at_place(place):
        dz, dy, flip = place
        return far_z[dz] + far_y[dy] + far_core[flip]

    def device(goal, plane):
        return {"mom": goal, "tm": plane}

    small = [
        pltpu.make_async_copy(source, target, load_sem.at[4 + number])
        for number, (source, target) in enumerate(
            ((prop_hbm, prop), (coup_hbm, coup), (mf_hbm, mf), (lag_hbm, lag))
        )
    ]
    loads = [
        pltpu.make_async_copy(hl, hlv.at[:, :, :, pl.ds(LANES, BLOCKS * LANES)], load_sem.at[0]),
        pltpu.make_async_copy(hr, hrv.at[:, :, :, pl.ds(LANES, BLOCKS * LANES)], load_sem.at[1]),
    ]
    tables_in = [
        pltpu.make_async_copy(ahead_hbm, ahead, load_sem.at[2]),
        pltpu.make_async_copy(back_hbm, backward, load_sem.at[3]),
    ]

    for load in small + loads + tables_in:
        load.start()
    barrier = pltpu.get_barrier_semaphore()

    def greet(goal, plane):
        pl.semaphore_signal(barrier, inc=1, device_id=device(goal, plane), device_id_type=MESH)

    for place in PLACES[:-1]:
        greet(at_place(place), x)

    @pl.when(x > 0)
    def _():
        greet(dev, x - 1)

    @pl.when(x == last)
    def _():
        for plane in range(last - 1):
            greet(dev, plane)

    for load in small:
        load.wait()

    lane = lax.broadcasted_iota(jnp.int32, (1, LANES), 1)
    low_half = lane < HALF
    even_block = lax.rem(lane // QUARTER, 2) == 0

    column = lax.broadcasted_iota(jnp.int32, (QUARTER, K), 0)
    point = lax.broadcasted_iota(jnp.int32, (QUARTER, K), 1)
    strength = jnp.zeros((QUARTER, K), F32)
    mf_term = jnp.zeros((QUARTER, K), F32)
    for b in range(ORB):
        here = lax.rem(column, ORB) == b
        strength = jnp.where(here, coup[row * ORB + b], strength)
        mf_term = jnp.where(here, mf[row * ORB + b], mf_term)
    strength = strength * strength
    mf_term = jnp.where((point == PAIRS) & (column >= ORB) & (quarter == 3), mf_term, 0.0)
    lone = lane >= PAIRS

    def transpose_blocks(parts):
        def swap_halves(a, b):
            moved = pltpu.roll(jnp.where(low_half, b, a), HALF, 1)
            return jnp.where(low_half, a, moved), jnp.where(low_half, moved, b)

        def swap_blocks(a, b):
            moving = jnp.where(even_block, b, a)
            moved = jnp.where(
                even_block, pltpu.roll(moving, LANES - QUARTER, 1), pltpu.roll(moving, QUARTER, 1)
            )
            return jnp.where(even_block, a, moved), jnp.where(even_block, moved, b)

        a, c = swap_halves(parts[0], parts[2])
        b, d = swap_halves(parts[1], parts[3])
        return [*swap_blocks(a, b), *swap_blocks(c, d)]

    def start_block(block):
        at = pl.ds(block * LANES, LANES)
        for k in range(HERE):
            stack = jnp.concatenate([prop[0, k], prop[1, k]], axis=0)
            real, imag = (
                jnp.dot(
                    stack, hlv[c, k, :, pl.ds((block + 1) * LANES, LANES)],
                    precision=lax.Precision.HIGHEST, preferred_element_type=F32,
                )
                for c in range(2)
            )
            startv[0, k, :, at] = real[:ORB] - imag[ORB:]
            startv[1, k, :, at] = real[ORB:] + imag[:ORB]

    def build(k, slot, source_r, source_l, lanes_from):
        for lp, source in enumerate((source_r, source_l)):
            for c in range(2):
                first = source[c, k, :, pl.ds(lanes_from, LANES)]
                second = source[c, k, :, pl.ds(lanes_from + LANES, LANES)]
                for m in range(W):
                    shift = ORB * (m + 1)
                    if shift < LANES:
                        moved = pltpu.roll(jnp.where(lane >= shift, first, second), LANES - shift, 1)
                    else:
                        moved = second
                    high, low = split(moved * lag[m])
                    at = lp * LANES + m * ORB
                    hank[slot, 0, pl.ds(at, ORB), pl.ds(c * LANES, LANES)] = high
                    hank[slot, 1, pl.ds(at, ORB), pl.ds(c * LANES, LANES)] = low

    def build_blocks(blocks):
        @pl.loop(0, HERE)
        def _(k):
            for block in blocks:
                build(k, block * HERE + k, hrv, hlv, block * LANES)

    def pack_window(p, reals, imags):
        for r in range(2):
            parts = transpose_blocks([reals[r], imags[r], reals[r + 2], imags[r + 2]])
            for w in range(4):
                sendf[p, pl.ds(2 * w + r, ORB, stride=8), :] = parts[w]

    def forward_copy(p, place, plane):
        goal = at_place(place)
        return pltpu.make_async_remote_copy(
            src_ref=sendf.at[p, pl.ds(goal * 2, 2), :], dst_ref=fbuf.at[p, pl.ds(dev * 2, 2), :],
            send_sem=f_send.at[p], recv_sem=f_recv.at[p],
            device_id=device(goal, plane), device_id_type=MESH,
        )

    def own_forward(p):
        here = pl.ds(dev * 2, 2)
        return pltpu.make_async_copy(sendf.at[p, here, :], fbuf.at[p, here, :], f_own.at[p])

    def back_copy(p, place):
        goal = at_place(place)
        return pltpu.make_async_remote_copy(
            src_ref=sendb.at[p, pl.ds(goal * HERE, HERE), :], dst_ref=rbuf.at[p, pl.ds(dev * HERE, HERE), :],
            send_sem=b_send.at[p], recv_sem=b_recv.at[p],
            device_id=device(goal, x), device_id_type=MESH,
        )

    def own_back(p):
        here = pl.ds(dev * HERE, HERE)
        return pltpu.make_async_copy(sendb.at[p, here, :], rbuf.at[p, here, :], f_own.at[PASSES + p])

    def wait_rows(rows, sem):
        while rows:
            some = sendb.at[0, pl.ds(0, min(rows, K)), :]
            pltpu.make_async_copy(some, some, sem).wait()
            rows -= min(rows, K)

    def send_forward(p):
        if p == PASSES - 1:
            pl.semaphore_wait(ready, last)
            for plane in range(last):
                for place in PLACES:
                    forward_copy(p, place, plane).start()
        own_forward(p).start()
        for place in PLACES[:-1]:
            forward_copy(p, place, last).start()

    def wait_forward(p):
        own_forward(p).wait()
        wait_rows(others * 2, f_recv.at[p])

    def real_space(p):
        turned = fbuf[p].T
        value = jnp.concatenate([turned[:HALF], turned[HALF:]], axis=1)
        high, low = split(value)
        product = mm(jnp.concatenate([high, low], axis=0), ahead[0])
        product = product[:HALF] + product[HALF:] + mm(high, ahead[1])
        even, odd = product[:, :LANES], product[:, LANES:]
        crossed = jnp.concatenate([-odd[QUARTER:], odd[:QUARTER]], axis=0)
        pos = jnp.concatenate(
            [jnp.where(lone, even, even + crossed), jnp.where(lone, odd, even - crossed)], axis=1
        )
        real, imag = pos[:QUARTER], pos[QUARTER:]
        square_real, square_imag = real * real, imag * imag
        factor = strength * (square_real + square_imag) + mf_term
        twice = 2.0 * strength
        both = jnp.concatenate(
            [factor * real, factor * imag, strength * (square_real - square_imag), twice * real * imag],
            axis=0,
        )
        first, second = both[:, :LANES], both[:, LANES:]
        change = first - second
        crossed = jnp.concatenate(
            [
                change[QUARTER : 2 * QUARTER],
                -change[:QUARTER],
                change[3 * QUARTER :],
                -change[2 * QUARTER : 3 * QUARTER],
            ],
            axis=0,
        )
        value = jnp.concatenate(
            [jnp.where(lone, first, first + second), jnp.where(lone, second, crossed)], axis=1
        )
        high, low = split(value)
        product = mm(jnp.concatenate([high, low], axis=0), backward[0])
        product = product[:LANES] + product[LANES:] + mm(high, backward[1])
        sendb[p, pl.ds(0, LANES), :] = product[:, :LANES].T
        sendb[p, pl.ds(LANES, LANES), :] = product[:, LANES:].T

    def send_back(p):
        own_back(p).start()
        for place in PLACES[:-1]:
            back_copy(p, place).start()

    def wait_back(p):
        own_back(p).wait()
        wait_rows(others * HERE, b_recv.at[p])

    def arrived(p, k):
        parts = transpose_blocks([rbuf[p, pl.ds(w * HERE + k, ORB, stride=4 * HERE), :] for w in range(4)])
        lesser_real, lesser_imag, pair_real, pair_imag = parts
        high, low = split(
            jnp.concatenate(
                [
                    jnp.concatenate([lesser_real, pair_real], axis=1),
                    jnp.concatenate([lesser_imag, pair_imag], axis=1),
                ],
                axis=0,
            )
        )
        return jnp.concatenate([high, low], axis=0)

    def collide(stack, slot):
        rows = 2 * ORB
        product = mm(stack, hank[slot, 0])
        total = product[:rows] + product[rows:] + mm(stack[:rows], hank[slot, 1])
        real = total[:ORB, :LANES] - total[ORB:, LANES:]
        imag = total[:ORB, LANES:] + total[ORB:, :LANES]
        return real, imag

    def rim_copy(part):
        src, dst = ((hl, hlv), (hr, hrv))[part]
        return pltpu.make_async_remote_copy(
            src_ref=src.at[:, :, :, pl.ds((BLOCKS - 1) * LANES, LANES)],
            dst_ref=dst.at[:, :, :, pl.ds(0, LANES)],
            send_sem=x_send.at[part], recv_sem=x_recv.at[part],
            device_id=device(dev, lax.rem(x + 1, TM)), device_id_type=MESH,
        )

    for load in loads:
        load.wait()
    start_block(BLOCKS - 1)
    newest_times = pl.ds((BLOCKS - 1) * LANES, LANES)

    @pl.when(x == last)
    def _():
        pack_window(0, *([startv[c, k, :, newest_times] for k in range(HERE)] for c in range(2)))
        pl.semaphore_wait(barrier, others)
        send_forward(0)

    @pl.when(x == last - 1)
    def _():
        pl.semaphore_wait(barrier, others + 1)

    @pl.when(x < last - 1)
    def _():
        pl.semaphore_wait(barrier, others + 2)

    @pl.when(x < last)
    def _():
        pl.semaphore_signal(ready, inc=1, device_id=device(dev, last), device_id_type=MESH)
        for part in range(2):
            rim_copy(part).start()

    @pl.when(x == 0)
    def _():
        zeros = jnp.zeros((2, HERE, ORB, LANES), F32)
        hlv[:, :, :, pl.ds(0, LANES)] = zeros
        hrv[:, :, :, pl.ds(0, LANES)] = zeros

    build_blocks((BLOCKS - 1,))
    for block in range(BLOCKS - 1):
        start_block(block)
    for load in tables_in:
        load.wait()

    @pl.when(x == last)
    def _():
        for p in range(PASSES - 1):
            if p:
                build_blocks((2,))
            wait_forward(p)
            real_space(p)
            send_back(p)
            if p == 0:
                build_blocks((1,))
            wait_back(p)
            reals, imags = [], []
            for k in range(HERE):
                real, imag = collide(arrived(p, k), (BLOCKS - 1) * HERE + k)
                reals.append(startv[0, k, :, newest_times] + imag)
                imags.append(startv[1, k, :, newest_times] - real)
            pack_window(p + 1, reals, imags)
            send_forward(p + 1)

    @pl.when(x < last)
    def _():
        build_blocks((1, 2))

    @pl.when(x > 0)
    def _():
        for part in range(2):
            rim_copy(part).wait_recv()

    build_blocks((0,))

    p = PASSES - 1

    @pl.when(x == last)
    def _():
        wait_forward(p)

    @pl.when(x < last)
    def _():
        wait_rows((others + 1) * 2, f_recv.at[p])

    real_space(p)
    send_back(p)
    wait_back(p)
    for k in range(HERE):
        stack = arrived(p, k)
        for block in range(BLOCKS):
            real, imag = collide(stack, block * HERE + k)
            at = pl.ds(block * LANES, LANES)
            out[0, k, :, at] = startv[0, k, :, at] + imag
            out[1, k, :, at] = startv[1, k, :, at] - real

    wait_rows(others * HERE, b_send.at[p])

    @pl.when(x == last)
    def _():
        for p in range(PASSES - 1):
            wait_rows(others * HERE, b_send.at[p])
            wait_rows(others * 2, f_send.at[p])
        wait_rows((others + last * (others + 1)) * 2, f_send.at[PASSES - 1])

    @pl.when(x < last)
    def _():
        for part in range(2):
            rim_copy(part).wait_send()


def on_device(ahead, back, hist_lesser, hist_retarded, propagator, coupling, mf_weight, lag_weight):
    vmem = pl.BlockSpec(memory_space=pltpu.VMEM)
    hbm = pl.BlockSpec(memory_space=pltpu.HBM)
    padded = (2, HERE, ORB, (BLOCKS + 1) * LANES)
    return pl.pallas_call(
        kernel,
        out_shape=pltpu.VMEM(hist_lesser.shape, F32),
        in_specs=[hbm] * 8,
        out_specs=vmem,
        scratch_shapes=[
            pltpu.VMEM((2, HERE, ORB, ORB), F32),
            pltpu.SMEM((ORB * ORB,), F32),
            pltpu.SMEM((ORB * ORB,), F32),
            pltpu.SMEM((W,), F32),
            pltpu.VMEM(padded, F32),
            pltpu.VMEM(padded, F32),
            pltpu.VMEM((2, K, K), BF16),
            pltpu.VMEM((2, K, K), BF16),
            pltpu.VMEM((2, HERE, ORB, BLOCKS * LANES), F32),
            pltpu.VMEM((BLOCKS * HERE, 2, 2 * LANES, 2 * LANES), BF16),
            pltpu.VMEM((PASSES, K // 2, LANES), F32),
            pltpu.VMEM((PASSES, K // 2, LANES), F32),
            pltpu.VMEM((PASSES, K, LANES), F32),
            pltpu.VMEM((PASSES, K, LANES), F32),
            pltpu.SemaphoreType.DMA((8,)),
            pltpu.SemaphoreType.DMA((2,)),
            pltpu.SemaphoreType.DMA((2,)),
            pltpu.SemaphoreType.DMA((PASSES,)),
            pltpu.SemaphoreType.DMA((PASSES,)),
            pltpu.SemaphoreType.DMA((2 * PASSES,)),
            pltpu.SemaphoreType.DMA((PASSES,)),
            pltpu.SemaphoreType.DMA((PASSES,)),
            pltpu.SemaphoreType.REGULAR,
        ],
        compiler_params=pltpu.CompilerParams(
            collective_id=0, has_side_effects=True, vmem_limit_bytes=67043328 - 4 * math.prod(hist_lesser.shape)
        ),
    )(hist_lesser, hist_retarded, propagator, coupling, mf_weight, lag_weight, ahead, back)


def solution(mesh):
    tables = momentum_tables()

    def step(*args):
        return jax.shard_map(
            on_device,
            mesh=mesh,
            in_specs=(
                P(None, None, None),
                P(None, None, None),
                P(None, "mom", None, "tm"),
                P(None, "mom", None, "tm"),
                P(None, "mom", None, None),
                P(),
                P(),
                P(),
            ),
            out_specs=P(None, "mom", None, "tm"),
            check_vma=False,
        )(*map(jnp.asarray, tables), *args)

    return step
```

```python
import math

import jax
import jax.numpy as jnp
import ml_dtypes
import numpy as np
from jax import lax
from jax.experimental import pallas as pl
from jax.experimental.pallas import tpu as pltpu
from jax.sharding import PartitionSpec as P

KX = 16
KY = 16
K = KX * KY
ORB = 16
W = 8
PASSES = 3
NZ, NY = 8, 4
CHIPS = NZ * NY
CORES = 2
TM = 4
HERE = 4
LANES = W * ORB
QUARTER = LANES // 4
HALF = LANES // 2
BLOCKS = 4

MESH = pl.DeviceIdType.MESH
F32 = jnp.float32
BF16 = jnp.bfloat16


PAIRS = K // 2 - 2


def momentum_tables():
    place = np.arange(K)
    parted = 4 * (place // 2 % (K // 4)) + place % 2 + 2 * (place // (K // 2))
    minus = (-(place // KY)) % KX * KY + (-(place % KY)) % KY
    alone = place[minus == place]
    upper = place[place < minus]

    def waves(rows, columns):
        turn = (rows[:, None] // KY) * (columns[None, :] // KY) % KX
        turn = turn + (rows[:, None] % KY) * (columns[None, :] % KY) % KY
        phase = 2.0 * math.pi * turn / 16.0
        return np.cos(phase) / 16.0, np.sin(phase) / 16.0

    def table(momenta):
        cosine, sine = waves(upper, momenta)
        lone = waves(alone, momenta)[0]
        return np.concatenate([cosine, lone[:2], sine, lone[2:]], axis=0).astype(np.float32)

    def parts(full):
        high = full.astype(ml_dtypes.bfloat16)
        low = (full - high.astype(np.float32)).astype(ml_dtypes.bfloat16)
        return np.stack([high, low])

    return parts(table(parted).T), parts(table(place))


def split(x):
    high = x.astype(BF16)
    return high, (x - high.astype(F32)).astype(BF16)


def mm(a, b):
    return jnp.dot(a, b, preferred_element_type=F32)


def ring(step, size):
    return min(step % size, -step % size)


PLACES = [
    (dz, dy, flip)
    for dz, dy in sorted(
        ((dz, dy) for dz in range(NZ) for dy in range(NY)), key=lambda o: -(ring(o[0], NZ) + ring(o[1], NY))
    )
    for flip in (1, 0)
]


def kernel(
    hl, hr, prop_hbm, coup_hbm, mf_hbm, lag_hbm, ahead_hbm, back_hbm,
    out,
    prop, coup, mf, lag, hlv, hrv, ahead, backward, startv, hank, sendf, fbuf, sendb, rbuf,
    load_sem, x_send, x_recv, f_send, f_recv, f_own, b_send, b_recv, ready,
):
    dev = lax.axis_index("mom")
    x = lax.axis_index("tm")
    core = lax.rem(dev, CORES)
    chip = dev // CORES
    z = chip // NY
    y = lax.rem(chip, NY)
    last = TM - 1
    others = CHIPS * CORES - 1
    row = chip // 2
    quarter = lax.rem(chip, 2) * 2 + core
    far_z = [lax.rem(z + dz, NZ) * (NY * CORES) for dz in range(NZ)]
    far_y = [lax.rem(y + dy, NY) * CORES for dy in range(NY)]
    far_core = [core, 1 - core]

    def at_place(place):
        dz, dy, flip = place
        return far_z[dz] + far_y[dy] + far_core[flip]

    def device(goal, plane):
        return {"mom": goal, "tm": plane}

    barrier = pltpu.get_barrier_semaphore()

    def greet(goal, plane):
        pl.semaphore_signal(barrier, inc=1, device_id=device(goal, plane), device_id_type=MESH)

    for place in PLACES[:-1]:
        greet(at_place(place), x)

    @pl.when(x > 0)
    def _():
        greet(dev, x - 1)

    @pl.when(x == last)
    def _():
        for plane in range(last - 1):
            greet(dev, plane)

    small = [
        pltpu.make_async_copy(source, target, load_sem.at[4 + number])
        for number, (source, target) in enumerate(
            ((prop_hbm, prop), (coup_hbm, coup), (mf_hbm, mf), (lag_hbm, lag))
        )
    ]
    loads = [
        pltpu.make_async_copy(hl, hlv.at[:, :, :, pl.ds(LANES, BLOCKS * LANES)], load_sem.at[0]),
        pltpu.make_async_copy(hr, hrv.at[:, :, :, pl.ds(LANES, BLOCKS * LANES)], load_sem.at[1]),
    ]
    tables_in = [
        pltpu.make_async_copy(ahead_hbm, ahead, load_sem.at[2]),
        pltpu.make_async_copy(back_hbm, backward, load_sem.at[3]),
    ]

    for load in small + loads + tables_in:
        load.start()
    for load in small:
        load.wait()

    lane = lax.broadcasted_iota(jnp.int32, (1, LANES), 1)
    block_of_lane = lane // QUARTER

    column = lax.broadcasted_iota(jnp.int32, (QUARTER, K), 0)
    point = lax.broadcasted_iota(jnp.int32, (QUARTER, K), 1)
    strength = jnp.zeros((QUARTER, K), F32)
    mf_term = jnp.zeros((QUARTER, K), F32)
    for b in range(ORB):
        here = lax.rem(column, ORB) == b
        strength = jnp.where(here, coup[row * ORB + b], strength)
        mf_term = jnp.where(here, mf[row * ORB + b], mf_term)
    strength = strength * strength
    mf_term = jnp.where((point == PAIRS) & (column >= ORB) & (quarter == 3), mf_term, 0.0)
    lone = lane >= PAIRS

    def transpose_blocks(parts):
        result = []
        for j in range(4):
            total = parts[j]
            for i in range(4):
                if i == j:
                    continue
                moved = pltpu.roll(parts[i], (QUARTER * (i - j)) % LANES, 1)
                total = jnp.where(block_of_lane == i, moved, total)
            result.append(total)
        return result

    def start_block(block):
        at = pl.ds(block * LANES, LANES)
        for k in range(HERE):
            stack = jnp.concatenate([prop[0, k], prop[1, k]], axis=0)
            real, imag = (
                jnp.dot(
                    stack, hlv[c, k, :, pl.ds((block + 1) * LANES, LANES)],
                    precision=lax.Precision.HIGHEST, preferred_element_type=F32,
                )
                for c in range(2)
            )
            startv[0, k, :, at] = real[:ORB] - imag[ORB:]
            startv[1, k, :, at] = real[ORB:] + imag[:ORB]

    def build(k, slot, source_r, source_l, lanes_from):
        for lp, source in enumerate((source_r, source_l)):
            for c in range(2):
                first = source[c, k, :, pl.ds(lanes_from, LANES)]
                second = source[c, k, :, pl.ds(lanes_from + LANES, LANES)]
                for m in range(W):
                    shift = ORB * (m + 1)
                    if shift < LANES:
                        moved = pltpu.roll(jnp.where(lane >= shift, first, second), LANES - shift, 1)
                    else:
                        moved = second
                    high, low = split(moved * lag[m])
                    at = lp * LANES + m * ORB
                    hank[slot, 0, pl.ds(at, ORB), pl.ds(c * LANES, LANES)] = high
                    hank[slot, 1, pl.ds(at, ORB), pl.ds(c * LANES, LANES)] = low

    def build_blocks(blocks):
        @pl.loop(0, HERE)
        def _(k):
            for block in blocks:
                build(k, block * HERE + k, hrv, hlv, block * LANES)

    def pack_window(p, reals, imags):
        for r in range(2):
            parts = transpose_blocks([reals[r], imags[r], reals[r + 2], imags[r + 2]])
            for w in range(4):
                sendf[p, pl.ds(2 * w + r, ORB, stride=8), :] = parts[w]

    def forward_copy(p, place, plane):
        goal = at_place(place)
        return pltpu.make_async_remote_copy(
            src_ref=sendf.at[p, pl.ds(goal * 2, 2), :], dst_ref=fbuf.at[p, pl.ds(dev * 2, 2), :],
            send_sem=f_send.at[p], recv_sem=f_recv.at[p],
            device_id=device(goal, plane), device_id_type=MESH,
        )

    def own_forward(p):
        here = pl.ds(dev * 2, 2)
        return pltpu.make_async_copy(sendf.at[p, here, :], fbuf.at[p, here, :], f_own.at[p])

    def back_copy(p, place):
        goal = at_place(place)
        return pltpu.make_async_remote_copy(
            src_ref=sendb.at[p, pl.ds(goal * HERE, HERE), :], dst_ref=rbuf.at[p, pl.ds(dev * HERE, HERE), :],
            send_sem=b_send.at[p], recv_sem=b_recv.at[p],
            device_id=device(goal, x), device_id_type=MESH,
        )

    def own_back(p):
        here = pl.ds(dev * HERE, HERE)
        return pltpu.make_async_copy(sendb.at[p, here, :], rbuf.at[p, here, :], f_own.at[PASSES + p])

    def wait_rows(rows, sem):
        while rows:
            some = sendb.at[0, pl.ds(0, min(rows, K)), :]
            pltpu.make_async_copy(some, some, sem).wait()
            rows -= min(rows, K)

    def send_forward(p):
        if p == PASSES - 1:
            pl.semaphore_wait(ready, last)
            for plane in range(last):
                for place in PLACES:
                    forward_copy(p, place, plane).start()
        own_forward(p).start()
        for place in PLACES[:-1]:
            forward_copy(p, place, last).start()

    def wait_forward(p):
        own_forward(p).wait()
        wait_rows(others * 2, f_recv.at[p])

    def real_space(p):
        turned = fbuf[p].T
        value = jnp.concatenate([turned[:HALF], turned[HALF:]], axis=1)
        high, low = split(value)
        product = mm(jnp.concatenate([high, low], axis=0), ahead[0])
        product = product[:HALF] + product[HALF:] + mm(high, ahead[1])
        even, odd = product[:, :LANES], product[:, LANES:]
        crossed = jnp.concatenate([-odd[QUARTER:], odd[:QUARTER]], axis=0)
        pos = jnp.concatenate(
            [jnp.where(lone, even, even + crossed), jnp.where(lone, odd, even - crossed)], axis=1
        )
        real, imag = pos[:QUARTER], pos[QUARTER:]
        square_real, square_imag = real * real, imag * imag
        factor = strength * (square_real + square_imag) + mf_term
        twice = 2.0 * strength
        both = jnp.concatenate(
            [factor * real, factor * imag, strength * (square_real - square_imag), twice * real * imag],
            axis=0,
        )
        first, second = both[:, :LANES], both[:, LANES:]
        change = first - second
        crossed = jnp.concatenate(
            [
                change[QUARTER : 2 * QUARTER],
                -change[:QUARTER],
                change[3 * QUARTER :],
                -change[2 * QUARTER : 3 * QUARTER],
            ],
            axis=0,
        )
        value = jnp.concatenate(
            [jnp.where(lone, first, first + second), jnp.where(lone, second, crossed)], axis=1
        )
        high, low = split(value)
        product = mm(jnp.concatenate([high, low], axis=0), backward[0])
        product = product[:LANES] + product[LANES:] + mm(high, backward[1])
        sendb[p, pl.ds(0, LANES), :] = product[:, :LANES].T
        sendb[p, pl.ds(LANES, LANES), :] = product[:, LANES:].T

    def send_back(p):
        own_back(p).start()
        for place in PLACES[:-1]:
            back_copy(p, place).start()

    def wait_back(p):
        own_back(p).wait()
        wait_rows(others * HERE, b_recv.at[p])

    def arrived(p, k):
        parts = transpose_blocks([rbuf[p, pl.ds(w * HERE + k, ORB, stride=4 * HERE), :] for w in range(4)])
        lesser_real, lesser_imag, pair_real, pair_imag = parts
        high, low = split(
            jnp.concatenate(
                [
                    jnp.concatenate([lesser_real, pair_real], axis=1),
                    jnp.concatenate([lesser_imag, pair_imag], axis=1),
                ],
                axis=0,
            )
        )
        return jnp.concatenate([high, low], axis=0)

    def collide(stack, slot):
        rows = 2 * ORB
        product = mm(stack, hank[slot, 0])
        total = product[:rows] + product[rows:] + mm(stack[:rows], hank[slot, 1])
        real = total[:ORB, :LANES] - total[ORB:, LANES:]
        imag = total[:ORB, LANES:] + total[ORB:, :LANES]
        return real, imag

    def rim_copy(part):
        src, dst = ((hl, hlv), (hr, hrv))[part]
        return pltpu.make_async_remote_copy(
            src_ref=src.at[:, :, :, pl.ds((BLOCKS - 1) * LANES, LANES)],
            dst_ref=dst.at[:, :, :, pl.ds(0, LANES)],
            send_sem=x_send.at[part], recv_sem=x_recv.at[part],
            device_id=device(dev, lax.rem(x + 1, TM)), device_id_type=MESH,
        )

    for load in loads:
        load.wait()
    start_block(BLOCKS - 1)
    newest_times = pl.ds((BLOCKS - 1) * LANES, LANES)

    @pl.when(x == last)
    def _():
        pack_window(0, *([startv[c, k, :, newest_times] for k in range(HERE)] for c in range(2)))
        pl.semaphore_wait(barrier, others)
        send_forward(0)

    @pl.when(x == last - 1)
    def _():
        pl.semaphore_wait(barrier, others + 1)

    @pl.when(x < last - 1)
    def _():
        pl.semaphore_wait(barrier, others + 2)

    @pl.when(x < last)
    def _():
        pl.semaphore_signal(ready, inc=1, device_id=device(dev, last), device_id_type=MESH)
        for part in range(2):
            rim_copy(part).start()

    @pl.when(x == 0)
    def _():
        zeros = jnp.zeros((2, HERE, ORB, LANES), F32)
        hlv[:, :, :, pl.ds(0, LANES)] = zeros
        hrv[:, :, :, pl.ds(0, LANES)] = zeros

    build_blocks((BLOCKS - 1,))
    for block in range(BLOCKS - 1):
        start_block(block)
    for load in tables_in:
        load.wait()

    @pl.when(x == last)
    def _():
        for p in range(PASSES - 1):
            if p:
                build_blocks((2,))
            wait_forward(p)
            real_space(p)
            send_back(p)
            if p == 0:
                build_blocks((1,))
            wait_back(p)
            reals, imags = [], []
            for k in range(HERE):
                real, imag = collide(arrived(p, k), (BLOCKS - 1) * HERE + k)
                reals.append(startv[0, k, :, newest_times] + imag)
                imags.append(startv[1, k, :, newest_times] - real)
            pack_window(p + 1, reals, imags)
            send_forward(p + 1)

    @pl.when(x < last)
    def _():
        build_blocks((1, 2))

    @pl.when(x > 0)
    def _():
        for part in range(2):
            rim_copy(part).wait_recv()

    build_blocks((0,))

    p = PASSES - 1

    @pl.when(x == last)
    def _():
        wait_forward(p)

    @pl.when(x < last)
    def _():
        wait_rows((others + 1) * 2, f_recv.at[p])

    real_space(p)
    send_back(p)
    wait_back(p)
    for k in range(HERE):
        stack = arrived(p, k)
        for block in range(BLOCKS):
            real, imag = collide(stack, block * HERE + k)
            at = pl.ds(block * LANES, LANES)
            out[0, k, :, at] = startv[0, k, :, at] + imag
            out[1, k, :, at] = startv[1, k, :, at] - real

    wait_rows(others * HERE, b_send.at[p])

    @pl.when(x == last)
    def _():
        for p in range(PASSES - 1):
            wait_rows(others * HERE, b_send.at[p])
            wait_rows(others * 2, f_send.at[p])
        wait_rows((others + last * (others + 1)) * 2, f_send.at[PASSES - 1])

    @pl.when(x < last)
    def _():
        for part in range(2):
            rim_copy(part).wait_send()


def on_device(ahead, back, hist_lesser, hist_retarded, propagator, coupling, mf_weight, lag_weight):
    vmem = pl.BlockSpec(memory_space=pltpu.VMEM)
    hbm = pl.BlockSpec(memory_space=pltpu.HBM)
    padded = (2, HERE, ORB, (BLOCKS + 1) * LANES)
    return pl.pallas_call(
        kernel,
        out_shape=pltpu.VMEM(hist_lesser.shape, F32),
        in_specs=[hbm] * 8,
        out_specs=vmem,
        scratch_shapes=[
            pltpu.VMEM((2, HERE, ORB, ORB), F32),
            pltpu.SMEM((ORB * ORB,), F32),
            pltpu.SMEM((ORB * ORB,), F32),
            pltpu.SMEM((W,), F32),
            pltpu.VMEM(padded, F32),
            pltpu.VMEM(padded, F32),
            pltpu.VMEM((2, K, K), BF16),
            pltpu.VMEM((2, K, K), BF16),
            pltpu.VMEM((2, HERE, ORB, BLOCKS * LANES), F32),
            pltpu.VMEM((BLOCKS * HERE, 2, 2 * LANES, 2 * LANES), BF16),
            pltpu.VMEM((PASSES, K // 2, LANES), F32),
            pltpu.VMEM((PASSES, K // 2, LANES), F32),
            pltpu.VMEM((PASSES, K, LANES), F32),
            pltpu.VMEM((PASSES, K, LANES), F32),
            pltpu.SemaphoreType.DMA((8,)),
            pltpu.SemaphoreType.DMA((2,)),
            pltpu.SemaphoreType.DMA((2,)),
            pltpu.SemaphoreType.DMA((PASSES,)),
            pltpu.SemaphoreType.DMA((PASSES,)),
            pltpu.SemaphoreType.DMA((2 * PASSES,)),
            pltpu.SemaphoreType.DMA((PASSES,)),
            pltpu.SemaphoreType.DMA((PASSES,)),
            pltpu.SemaphoreType.REGULAR,
        ],
        compiler_params=pltpu.CompilerParams(
            collective_id=0, has_side_effects=True, vmem_limit_bytes=67043328 - 4 * math.prod(hist_lesser.shape)
        ),
    )(hist_lesser, hist_retarded, propagator, coupling, mf_weight, lag_weight, ahead, back)


def solution(mesh):
    tables = momentum_tables()

    def step(*args):
        return jax.shard_map(
            on_device,
            mesh=mesh,
            in_specs=(
                P(None, None, None),
                P(None, None, None),
                P(None, "mom", None, "tm"),
                P(None, "mom", None, "tm"),
                P(None, "mom", None, None),
                P(),
                P(),
                P(),
            ),
            out_specs=P(None, "mom", None, "tm"),
            check_vma=False,
        )(*map(jnp.asarray, tables), *args)

    return step
```
